128 devices in a mesh: clip: 32 (over z_hi, y, x), head: 4 (over z_lo, core).
Axes of the slice: x: 4, y: 4, z: 4 (z_hi: 2, z_lo: 2; z = z_hi * 2 + z_lo), core: 2. Of those that a mesh axis runs over, the one named last changes fastest.
Arguments:
- video: bfloat16 [16384, 3072], P(('clip', 'head')), may hold values from -6 to 6
- norm_gain: float32 [2, 3072], replicated, may hold values from 0.25 to 1.75
- w_qkv: bfloat16 [2, 3072, 3, 1536], P(None, None, None, 'head'), may hold values from -0.109375 to 0.109375
- qk_gain: float32 [2, 2, 128], replicated, may hold values from 0.5 to 2
- w_out: bfloat16 [2, 1536, 3072], P(None, 'head'), may hold values from -0.875 to 0.875
- skip_layer: int32 [64], P('clip'), may hold values from 0 to 1
- halo_frames: int32 [64], P('clip'), may hold values from 1 to 2, as said below
- context_index: int32 [64, 8], P('clip'), may hold values from 0 to 255, as said below
Outputs:
- guided: bfloat16 [16384, 3072], P(('clip', 'head'))
The draws below stay inside these ranges and needn't reach their ends.
Inputs may be any that keep to these rules, and one draw needn't show every extreme that they name: `halo_frames`: every draw holds a clip with 2 and a clip with 1. `context_index`: within a clip the indices increase, one in each run of 32 positions.
All inputs are finite; a program needn't handle non-finite values.
Results may differ from the reference program's by a relative error of at most 0.028.
Values may be sent and summed in bfloat16 or wider, within the bound.
No kernel may reach another device: no remote copies, remote signals or barrier semaphores. Data moves between devices by JAX's collectives and lax.ppermute only.
A program may use at most 128 MiB of HBM per device.

```python
import math
import jax
import jax.numpy as jnp
from jax import lax

D = 3072
HD = 128
HEADS = 12
LAYERS = 2
FRAMES = 16
FRAME_TOK = 16
CTX = 8
HALO_F = 2
GROUPS = 4
CLIP_TOK = 256
CLIPS = 64
TOKENS = 16384


def draw_halo_frames(key, part):
    counts = jax.random.randint(key, (CLIPS,), 1, HALO_F + 1).astype(jnp.int32)
    where_top = jax.random.randint(jax.random.fold_in(key, 7), (), 0, CLIPS)
    counts = counts.at[where_top].set(HALO_F)
    counts = counts.at[(where_top + 1) % CLIPS].set(1)
    return counts.astype(jnp.int32)


def draw_context_index(key, part):
    stride = CLIP_TOK // CTX
    offsets = jax.random.randint(key, (CLIPS, CTX), 0, stride).astype(jnp.int32)
    chosen = jnp.arange(CTX, dtype=jnp.int32)[None, :] * stride + offsets
    chosen = chosen.at[0, 0].set(0)
    chosen = chosen.at[0, CTX - 1].set(CLIP_TOK - 1)
    return chosen.astype(jnp.int32)


def set_ends(array, rng, low, largest):
    place = [jax.random.randint(jax.random.fold_in(rng, axis), (), 0, length) for axis, length in enumerate(array.shape)]
    widest = array.shape.index(max(array.shape))
    beside = place[:widest] + [(place[widest] + 1) % array.shape[widest]] + place[widest + 1:]
    return array.at[tuple(place)].set(low).at[tuple(beside)].set(largest)


def block_levels(own_key, dims, cuts, smallest, top_value):
    def one(dim, blocks):
        draws = jax.random.uniform(jax.random.fold_in(jax.random.fold_in(own_key, 6), dim), (blocks,), jnp.float32, smallest / len(cuts), top_value / len(cuts))
        return jnp.repeat(jnp.exp(draws), dims[dim] // blocks).reshape((-1,) + (1,) * (len(dims) - dim - 1))

    level = one(*cuts[0])
    for cut in cuts[1:]:
        level = level * one(*cut)
    return level


def noise(stream_key, dims, scale, most, pieces=(), kind=jnp.bfloat16):
    level = block_levels(stream_key, dims, pieces, -0.22, 0.18) if pieces else 1.0
    result = jax.random.normal(stream_key, dims, jnp.float32) * scale * level
    return jnp.minimum(jnp.maximum(result, -most), most).astype(kind)


def setup_inputs(seed: int = 0) -> dict:
    splits = jax.random.split(jax.random.key(seed), 9)
    video = noise(splits[0], (TOKENS, D), 1.0, 6.0, ((0, 128),))
    norm_gain = jnp.clip(1.0 + 0.15 * jax.random.normal(splits[1], (LAYERS, D), jnp.float32), 0.25, 1.75)
    w_qkv = noise(splits[2], (LAYERS, D, 3, HEADS * HD), D ** -0.5, 0.109375, ((3, 4),))
    qk_gain = jnp.clip(jnp.exp(jax.random.uniform(splits[3], (LAYERS, 2, HD), jnp.float32, math.log(0.5), math.log(2.0))), 0.5, 2.0)
    w_out = noise(splits[4], (LAYERS, HEADS * HD, D), (max(HEADS * HD // 32, 1)) ** -0.5, 0.875, ((1, 4),))
    skip_layer = set_ends(jax.random.randint(splits[5], (CLIPS,), 0, LAYERS), jax.random.fold_in(splits[5], 1), 0, LAYERS - 1).astype(jnp.int32)
    halo_frames = draw_halo_frames(jax.random.fold_in(splits[8], 71), 0)
    context_index = draw_context_index(jax.random.fold_in(splits[8], 71), 0)
    return dict(video=video, norm_gain=norm_gain, w_qkv=w_qkv, qk_gain=qk_gain, w_out=w_out, skip_layer=skip_layer, halo_frames=halo_frames, context_index=context_index)


GUIDE = 1.5

def rms_scale(values, gain):
    return values * lax.rsqrt(lax.optimization_barrier(jnp.mean(values * values, axis=-1, keepdims=True)) + 1e-06) * gain

def layer(tokens, gain, weight_qkv, gains_qk, weight_out, halo_frames, context_index):
    tokens_f = tokens.astype(jnp.float32)
    normed = rms_scale(tokens_f, gain).astype(jnp.bfloat16)
    inner = HEADS * HD
    projected = jnp.dot(normed, weight_qkv.reshape(D, 3 * inner), preferred_element_type=jnp.float32)
    projected = projected.reshape(TOKENS, 3, HEADS, HD)
    queries = rms_scale(projected[:, 0], gains_qk[0]).astype(jnp.bfloat16)
    keyset = rms_scale(projected[:, 1], gains_qk[1]).astype(jnp.bfloat16)
    valueset = projected[:, 2].astype(jnp.bfloat16)
    offsets = (jnp.arange(CLIPS, dtype=jnp.int32) * CLIP_TOK)[:, None]
    picked = (context_index.astype(jnp.int32) + offsets).reshape(-1)
    context_keys = jnp.take(keyset, picked, axis=0)
    context_values = jnp.take(valueset, picked, axis=0)
    blank = jnp.zeros((CLIP_TOK, HEADS, HD), jnp.bfloat16)
    padded_keys = jnp.concatenate([blank, keyset, blank], axis=0).reshape(CLIPS + 2, CLIP_TOK, HEADS, HD)
    padded_values = jnp.concatenate([blank, valueset, blank], axis=0).reshape(CLIPS + 2, CLIP_TOK, HEADS, HD)
    query_clips = queries.reshape(CLIPS, CLIP_TOK, HEADS, HD)
    places = jnp.arange(3 * CLIP_TOK, dtype=jnp.int32)
    which = places // CLIP_TOK
    key_frame = places % CLIP_TOK // FRAME_TOK
    scale = 1.0 / math.sqrt(HD)

    def one_clip(clip_id):
        query_rows = lax.dynamic_index_in_dim(query_clips, clip_id, 0, keepdims=False)
        near_keys = lax.dynamic_slice_in_dim(padded_keys, clip_id, 3, 0).reshape(3 * CLIP_TOK, HEADS, HD)
        near_values = lax.dynamic_slice_in_dim(padded_values, clip_id, 3, 0).reshape(3 * CLIP_TOK, HEADS, HD)
        seen = halo_frames[clip_id]
        global_clip = clip_id - 1 + which
        valid = (global_clip >= 0) & (global_clip < CLIPS) & ((which == 1) | (which == 0) & (key_frame >= FRAMES - seen) | (which == 2) & (key_frame < seen))
        allowed = jnp.concatenate([valid, jnp.ones((CLIPS * CTX,), dtype=bool)])
        key_rows = jnp.concatenate([near_keys, context_keys], axis=0).astype(jnp.float32)
        value_rows = jnp.concatenate([near_values, context_values], axis=0).astype(jnp.float32)
        scores = jnp.einsum('qhd,khd->hqk', query_rows.astype(jnp.float32), key_rows) * scale
        scores = jnp.where(allowed[None, None, :], scores, -1e+30)
        peak = lax.optimization_barrier(jnp.max(scores, axis=-1, keepdims=True))
        expo = jnp.where(allowed[None, None, :], jnp.exp(scores - peak), 0.0)
        weights = (expo / lax.optimization_barrier(jnp.sum(expo, axis=-1, keepdims=True))).astype(jnp.bfloat16)
        attended = jnp.einsum('hqk,khd->qhd', weights.astype(jnp.float32), value_rows)
        return attended.astype(jnp.bfloat16)
    attended = lax.map(one_clip, jnp.arange(CLIPS, dtype=jnp.int32)).reshape(TOKENS, inner)
    share = inner // GROUPS
    total = jnp.zeros((TOKENS, D), jnp.float32)
    for group in range(GROUPS):
        term = jnp.dot(attended[:, group * share:(group + 1) * share], weight_out[group * share:(group + 1) * share], preferred_element_type=jnp.float32)
        rounded = lax.optimization_barrier(term.astype(jnp.bfloat16))
        total = total + rounded.astype(jnp.float32)
    return (tokens_f + total).astype(jnp.bfloat16)

def reference(video, norm_gain, w_qkv, qk_gain, w_out, skip_layer, halo_frames, context_index):
    first = layer(video, norm_gain[0], w_qkv[0], qk_gain[0], w_out[0], halo_frames, context_index)
    strong = layer(first, norm_gain[1], w_qkv[1], qk_gain[1], w_out[1], halo_frames, context_index)
    other = layer(video, norm_gain[1], w_qkv[1], qk_gain[1], w_out[1], halo_frames, context_index)
    skip_rows = jnp.repeat(skip_layer.astype(jnp.int32), CLIP_TOK)
    weak = jnp.where((skip_rows == 0)[:, None], other, first)
    strong_f = strong.astype(jnp.float32)
    return (strong_f + GUIDE * (strong_f - weak.astype(jnp.float32))).astype(jnp.bfloat16)
```

```python
import functools
import math

import jax
import jax.numpy as jnp
from jax import lax
from jax.experimental import pallas as pl
from jax.experimental.pallas import tpu as pltpu
from jax.sharding import PartitionSpec as P

D = 3072
HD = 128
HL = 3
INNER = HL * HD
BLK = 128
CLIP_TOK = 256
CTX = 8
HALO = 32
QUART = D // 4
GUIDE = 1.5
EPS = 1e-06
AXES = ("clip", "head")
F32, BF16 = jnp.float32, jnp.bfloat16
ANY = pl.BlockSpec(memory_space=pl.ANY)
VM = pl.BlockSpec(memory_space=pltpu.VMEM)
SM = pl.BlockSpec(memory_space=pltpu.SMEM)
LIMIT = 56 * 1024 * 1024


def moved(clips, heads, rule):
    pairs = []
    for c in range(clips):
        for h in range(heads):
            to = rule(c, h)
            if to is not None:
                pairs.append((c * heads + h, to[0] * heads + to[1]))
    return pairs


def send(value, rule):
    pairs = moved(lax.axis_size("clip"), lax.axis_size("head"), rule)
    return lax.ppermute(value, AXES, pairs)


def to_sib(c, h):
    return c, h ^ 1


def to_z(c, h):
    return c, h ^ 2


def to_diag(c, h):
    return c, h ^ 3


def to_far_z(c, h):
    return c ^ 16, h ^ 2


def to_x(step):
    return lambda c, h: ((c & ~3) | ((c + step) & 3), h)


def to_y(step):
    return lambda c, h: ((c & ~12) | ((c + 4 * step) & 12), h)


def edge_own(c, h):
    to = c - 1 if h < 2 else c + 1
    return (to, h) if 0 <= to < 32 else None


def edge_par(c, h):
    to = c + 1 if h < 2 else c - 1
    return (to, h) if 0 <= to < 32 else None


def norm_rows(src, gain, dst, row0, rows):
    def step(i, carry):
        at = pl.ds(pl.multiple_of(i * 16, 16), 16)
        v = src[at, :].astype(F32)
        ms = jnp.mean(v * v, axis=-1, keepdims=True)
        to = pl.ds(pl.multiple_of(row0 + i * 16, 16), 16)
        dst[to, :] = (v * lax.rsqrt(ms + EPS) * gain[...]).astype(BF16)
        return carry

    lax.fori_loop(0, rows // 16, step, 0, unroll=2)


def head_norm(p, gain):
    parts = []
    for h in range(HL):
        ph = p[:, h * HD : (h + 1) * HD]
        ms = jnp.mean(ph * ph, axis=-1, keepdims=True)
        parts.append(ph * lax.rsqrt(ms + EPS) * gain)
    return jnp.concatenate(parts, axis=1)


def finish_part(c, p, qkg):
    if c < 2:
        return head_norm(p, qkg[c : c + 1, :]).astype(BF16)
    return p.astype(BF16)


def put_edges(sc, which, out, edge, ctx, ci):
    core = sc[0]
    parity = sc[1] if which == 0 else 1 - sc[1]
    for side in range(2):
        last = parity if side == 0 else 1 - parity
        start = pl.multiple_of((last ^ core) * BLK + last * (BLK - HALO), HALO)
        for kv in range(2):
            edge[side, kv] = out[1 + kv, pl.ds(start, HALO), :]
    idx = ci[...]
    rel = ((idx // BLK) ^ core) * BLK + idx % BLK
    hot = (lax.broadcasted_iota(jnp.int32, (CTX, CLIP_TOK), 1) == rel).astype(BF16)
    for kv in range(2):
        ctx[kv] = jnp.dot(hot, out[1 + kv], preferred_element_type=F32).astype(BF16)


def qkv_kernel(
    layer, which, sc, xa, xb, gain, w, qkg, ci, out, edge, ctx, xbuf, wbuf, normed, sems
):
    copies = [
        pltpu.make_async_copy(xa, xbuf.at[pl.ds(0, BLK)], sems.at[0]),
        pltpu.make_async_copy(xb, xbuf.at[pl.ds(BLK, BLK)], sems.at[1]),
    ]
    for c in range(3):
        copies.append(
            pltpu.make_async_copy(w.at[layer, c], wbuf.at[c], sems.at[2 + c])
        )
    for copy in copies:
        copy.start()
    copies[0].wait()
    copies[1].wait()
    norm_rows(xbuf, gain, normed, 0, CLIP_TOK)
    for c in range(3):
        copies[2 + c].wait()
        p = jnp.dot(normed[...], wbuf[c], preferred_element_type=F32)
        out[c] = finish_part(c, p, qkg)
    put_edges(sc, which, out, edge, ctx, ci)


def qkv(layer, which, sc, xa, xb, gain, w, qkg, ci):
    return pl.pallas_call(
        functools.partial(qkv_kernel, layer, which),
        out_shape=(
            jax.ShapeDtypeStruct((3, CLIP_TOK, INNER), BF16),
            jax.ShapeDtypeStruct((2, 2, HALO, INNER), BF16),
            jax.ShapeDtypeStruct((2, CTX, INNER), BF16),
        ),
        in_specs=[SM, ANY, ANY, VM, ANY, VM, VM],
        out_specs=(VM, VM, VM),
        scratch_shapes=[
            pltpu.VMEM((CLIP_TOK, D), BF16),
            pltpu.VMEM((3, D, INNER), BF16),
            pltpu.VMEM((CLIP_TOK, D), BF16),
            pltpu.SemaphoreType.DMA((5,)),
        ],
        compiler_params=pltpu.CompilerParams(vmem_limit_bytes=LIMIT),
        cost_estimate=pl.CostEstimate(
            flops=2 * CLIP_TOK * D * 3 * INNER,
            transcendentals=0,
            bytes_accessed=2 * (3 * D * INNER + CLIP_TOK * D),
        ),
        name="qkv",
    )(sc, xa, xb, gain, w, qkg, ci)


def attn_kernel(which, sc, mine, inner, outer, ctx, out):
    core = sc[0]
    parity = sc[1] if which == 0 else 1 - sc[1]
    seen = sc[2 + which]
    exists = sc[4 + which]
    lane = lax.broadcasted_iota(jnp.int32, (1, 2 * HALO), 1)
    mask = jnp.zeros((1, 2 * HALO), F32)
    for side, count in enumerate((seen, seen * exists)):
        prev = parity if side == 0 else 1 - parity
        low = side * HALO + prev * (HALO - 16 * count)
        mask = jnp.where(lane >= low, jnp.where(lane < low + 16 * count, 1.0, mask), mask)
    factor = math.log2(math.e) / math.sqrt(HD)
    tn = (((1,), (1,)), ((), ()))
    groups = ctx.shape[0]
    ctx_rows = groups * ctx.shape[2]
    for h in range(HL):
        cols = slice(h * HD, (h + 1) * HD)
        q = mine[0, :, cols]
        ck = ctx[:, 0, :, cols].reshape(ctx_rows, HD)
        cv = ctx[:, 1, :, cols].reshape(ctx_rows, HD)
        k = jnp.concatenate([mine[1, :, cols], ck], axis=0)
        v = jnp.concatenate([mine[2, :, cols], cv], axis=0)
        kh = jnp.concatenate([inner[0, :, cols], outer[0, :, cols]], axis=0)
        vh = jnp.concatenate([inner[1, :, cols], outer[1, :, cols]], axis=0)
        v = jnp.concatenate([v, jnp.ones_like(v)], axis=1)
        vh = jnp.concatenate([vh, jnp.ones_like(vh)], axis=1)
        s = lax.dot_general(q, k, tn, preferred_element_type=F32)
        sh = lax.dot_general(q, kh, tn, preferred_element_type=F32)
        p = jnp.exp2(s * factor).astype(BF16)
        ph = (jnp.exp2(sh * factor) * mask).astype(BF16)
        r = jnp.dot(p, v, preferred_element_type=F32)
        r = r + jnp.dot(ph, vh, preferred_element_type=F32)
        a = (r[:, :HD] / r[:, HD:]).astype(BF16)
        out[0, :, cols] = a[:BLK]
        out[1, :, cols] = a[BLK:]


def attend(which, sc, mine, inner, outer, ctx):
    keys = CLIP_TOK + 2 * HALO + ctx.shape[0] * ctx.shape[2]
    return pl.pallas_call(
        functools.partial(attn_kernel, which),
        out_shape=jax.ShapeDtypeStruct((2, BLK, INNER), BF16),
        in_specs=[SM, VM, VM, VM, VM],
        out_specs=VM,
        compiler_params=pltpu.CompilerParams(vmem_limit_bytes=LIMIT),
        cost_estimate=pl.CostEstimate(
            flops=6 * CLIP_TOK * keys * INNER,
            transcendentals=HL * CLIP_TOK * keys,
            bytes_accessed=4 * keys * INNER + 4 * CLIP_TOK * INNER,
        ),
        name="attend",
    )(sc, mine, inner, outer, ctx)


def weight_copies(layer, turn, wo, wsib, wz, wzs, wcat, sems):
    copies = [
        pltpu.make_async_copy(wo.at[layer], wcat.at[pl.ds(0, INNER)], sems.at[0]),
        pltpu.make_async_copy(wsib.at[layer], wcat.at[pl.ds(INNER, INNER)], sems.at[1]),
    ]
    for j, stack in enumerate((wz, wzs)):
        for k, off in enumerate((0, 3, 1, 2)):
            col = pl.multiple_of(((turn + off) & 3) * QUART, QUART)
            copies.append(
                pltpu.make_async_copy(
                    stack.at[k],
                    wcat.at[pl.ds((2 + j) * INNER, INNER), pl.ds(col, QUART)],
                    sems.at[2 + 4 * j + k],
                )
            )
    return copies


def first_kernel(*refs):
    (sc, o0, p0, o1, p1, o2, p2, o3, p3, x0, x1, x2, x3, wo, wsib, wz, wzs) = refs[:17]
    (gain, w, qkg, cio, cip) = refs[17:22]
    (first, outo, edgeo, ctxo, outp, edgep, ctxp) = refs[22:29]
    (acat, wcat, xbuf, wbuf, normed, asems, xsems, wsems, qsems) = refs[29:]
    xs = (x0, x1, x2, x3)
    copies = []
    for j, (ao, ap) in enumerate(((o0, p0), (o1, p1), (p2, o2), (p3, o3))):
        for clip, piece in enumerate((ao, ap)):
            for b in range(2):
                src = piece.at[b ^ (j & 1)]
                dst = acat.at[pl.ds((2 * clip + b) * BLK, BLK), pl.ds(j * INNER, INNER)]
                copies.append(
                    pltpu.make_async_copy(src, dst, asems.at[4 * j + 2 * clip + b])
                )
    copies += weight_copies(0, sc[6], wo, wsib, wz, wzs, wcat, wsems)
    for j in range(4):
        copies.append(
            pltpu.make_async_copy(xs[j], xbuf.at[pl.ds(j * BLK, BLK)], xsems.at[j])
        )
    late = [pltpu.make_async_copy(w.at[1, c], wbuf.at[c], qsems.at[c]) for c in range(3)]
    for copy in copies + late:
        copy.start()
    for copy in copies:
        copy.wait()
    rows = 2 * CLIP_TOK
    for n in range(D // 512):
        cols = slice(n * 512, (n + 1) * 512)
        t = jnp.dot(acat[...], wcat[:, cols], preferred_element_type=F32)
        xbuf[:, cols] = (xbuf[:, cols].astype(F32) + t).astype(BF16)
    first[...] = xbuf[pl.ds(0, BLK), :]
    norm_rows(xbuf, gain, normed, 0, rows)
    for c in range(3):
        late[c].wait()
        p = jnp.dot(normed[...], wbuf[c], preferred_element_type=F32)
        p = finish_part(c, p, qkg)
        outo[c] = p[:CLIP_TOK]
        outp[c] = p[CLIP_TOK:]
    put_edges(sc, 0, outo, edgeo, ctxo, cio)
    put_edges(sc, 1, outp, edgep, ctxp, cip)


def first_qkv(sc, atts, xs, wo, wsib, wz, wzs, gain, w, qkg, cio, cip):
    one = (
        jax.ShapeDtypeStruct((3, CLIP_TOK, INNER), BF16),
        jax.ShapeDtypeStruct((2, 2, HALO, INNER), BF16),
        jax.ShapeDtypeStruct((2, CTX, INNER), BF16),
    )
    rows = 2 * CLIP_TOK
    res = pl.pallas_call(
        first_kernel,
        out_shape=(jax.ShapeDtypeStruct((BLK, D), BF16),) + one + one,
        in_specs=[SM] + [ANY] * 8 + [ANY] * 4 + [ANY] * 4 + [VM, ANY, VM, VM, VM],
        out_specs=(VM,) * 7,
        scratch_shapes=[
            pltpu.VMEM((rows, 4 * INNER), BF16),
            pltpu.VMEM((4 * INNER, D), BF16),
            pltpu.VMEM((rows, D), BF16),
            pltpu.VMEM((3, D, INNER), BF16),
            pltpu.VMEM((rows, D), BF16),
            pltpu.SemaphoreType.DMA((16,)),
            pltpu.SemaphoreType.DMA((4,)),
            pltpu.SemaphoreType.DMA((10,)),
            pltpu.SemaphoreType.DMA((3,)),
        ],
        compiler_params=pltpu.CompilerParams(vmem_limit_bytes=LIMIT),
        cost_estimate=pl.CostEstimate(
            flops=2 * rows * D * 7 * INNER,
            transcendentals=0,
            bytes_accessed=2 * (7 * D * INNER + 2 * rows * D),
        ),
        name="first_qkv",
    )(sc, *atts, *xs, wo, wsib, wz, wzs, gain, w, qkg, cio, cip)
    return res[0], res[1:4], res[4:7]


def final_kernel(*refs):
    sc, atts, others = refs[0], refs[1:5], refs[5:9]
    (video, first, wo, wsib, wz, wzs, out, acat, wcat, asems, wsems) = refs[9:]
    copies = []
    for j in range(4):
        for b, piece in enumerate((atts[j], others[j])):
            dst = acat.at[pl.ds(b * BLK, BLK), pl.ds(j * INNER, INNER)]
            copies.append(pltpu.make_async_copy(piece, dst, asems.at[2 * j + b]))
    copies += weight_copies(1, sc[7], wo, wsib, wz, wzs, wcat, wsems)
    for copy in copies:
        copy.start()
    for copy in copies:
        copy.wait()
    skip_first = sc[8] == 0
    for n in range(D // 512):
        cols = slice(n * 512, (n + 1) * 512)
        t = jnp.dot(acat[...], wcat[:, cols], preferred_element_type=F32)
        f = first[:, cols].astype(F32)
        strong = (f + t[:BLK]).astype(BF16).astype(F32)
        other = (video[:, cols].astype(F32) + t[BLK:]).astype(BF16).astype(F32)
        weak = jnp.where(skip_first, other, f)
        out[:, cols] = (strong + GUIDE * (strong - weak)).astype(BF16)


def final(sc, atts, others, video, first, wo, wsib, wz, wzs):
    return pl.pallas_call(
        final_kernel,
        out_shape=jax.ShapeDtypeStruct((BLK, D), BF16),
        in_specs=[SM] + [ANY] * 8 + [VM, VM] + [ANY] * 4,
        out_specs=VM,
        scratch_shapes=[
            pltpu.VMEM((2 * BLK, 4 * INNER), BF16),
            pltpu.VMEM((4 * INNER, D), BF16),
            pltpu.SemaphoreType.DMA((8,)),
            pltpu.SemaphoreType.DMA((10,)),
        ],
        compiler_params=pltpu.CompilerParams(vmem_limit_bytes=LIMIT),
        cost_estimate=pl.CostEstimate(
            flops=4 * BLK * D * 4 * INNER,
            transcendentals=0,
            bytes_accessed=2 * (4 * D * INNER + 3 * BLK * D),
        ),
        name="final",
    )(sc, *atts, *others, video, first, wo, wsib, wz, wzs)


def everyone(shard):
    copies = jnp.broadcast_to(shard, (lax.axis_size("clip"), *shard.shape))
    return lax.all_to_all(copies, "clip", split_axis=0, concat_axis=0, tiled=True)


def gathered(weight, layer, turn, move):
    mine = lax.dynamic_slice(weight[layer], (0, turn * QUART), (INNER, QUART))
    here = send(mine, to_far_z)
    low = send(here, move(1))
    high = send(here, move(-1))
    half = INNER // 2
    top = send(high[:half], move(-1))
    bottom = send(low[half:], move(1))
    stack = jnp.stack([here, low, high, jnp.concatenate([top, bottom], axis=0)], axis=0)
    return stack, send(stack, to_sib)


def spread(own, par):
    outer_par = send(own[1][0], edge_own)
    outer_own = send(par[1][0], edge_par)
    ctx = everyone(jnp.concatenate([own[2], par[2]], axis=1))
    return outer_own, outer_par, ctx


def body(video, norm_gain, w_qkv, qk_gain, w_out, skip_layer, halo_frames, context_index):
    clip = lax.axis_index("clip").astype(jnp.int32)
    head = lax.axis_index("head").astype(jnp.int32)
    clips = lax.axis_size("clip")
    core, zlo = head % 2, head // 2
    not_first = (clip > 0).astype(jnp.int32)
    not_last = (clip < clips - 1).astype(jnp.int32)
    even = zlo == 0
    turn_x, turn_y = clip % 4, clip // 4 % 4
    sc = jnp.stack(
        [
            core,
            zlo,
            jnp.where(even, halo_frames[0], halo_frames[1]),
            jnp.where(even, halo_frames[1], halo_frames[0]),
            jnp.where(even, not_first, not_last),
            jnp.where(even, not_last, not_first),
            turn_x,
            turn_y,
            jnp.where(even, skip_layer[0], skip_layer[1]),
        ]
    ).astype(jnp.int32)
    ci_own = jnp.where(even, context_index[0], context_index[1])[:, None]
    ci_par = jnp.where(even, context_index[1], context_index[0])[:, None]
    w = jnp.transpose(w_qkv, (0, 2, 1, 3))
    gains = [norm_gain[0:1], norm_gain[1:2]]

    x0 = video
    x2 = send(x0, to_z)
    x1 = send(x0, to_sib)
    wsib = send(w_out, to_sib)
    wz0, wzs0 = gathered(w_out, 0, turn_x, to_x)
    x3 = send(x2, to_sib)
    wz1, wzs1 = gathered(w_out, 1, turn_y, to_y)

    own = [None, None]
    par = [None, None]
    own[0] = qkv(0, 0, sc, x0, x1, gains[0], w, qk_gain[0], ci_own)
    own[1] = qkv(1, 0, sc, x0, x1, gains[1], w, qk_gain[1], ci_own)
    par[0] = qkv(0, 1, sc, x2, x3, gains[0], w, qk_gain[0], ci_par)
    oo, op, ctx = spread(own[0], par[0])
    par[1] = qkv(1, 1, sc, x2, x3, gains[1], w, qk_gain[1], ci_par)
    ao = attend(0, sc, own[0][0], par[0][1][1], oo, ctx)
    ap = attend(1, sc, par[0][0], own[0][1][1], op, ctx)
    oz = send(ao, to_z)
    os = send(ao, to_sib)
    pz = send(ap, to_z)
    ps = send(ap, to_sib)
    ozs = send(oz, to_sib)
    pzs = send(pz, to_sib)

    woo, wop, wctx = spread(own[1], par[1])
    bo = attend(0, sc, own[1][0], par[1][1][1], woo, wctx)
    bp = attend(1, sc, par[1][0], own[1][1][1], wop, wctx)
    others = [bo[0], send(bo[1], to_sib), send(bp[0], to_z), send(bp[1], to_diag)]

    first, fo, fp = first_qkv(
        sc,
        (ao, ap, os, ps, oz, pz, ozs, pzs),
        (x0, x1, x2, x3),
        w_out,
        wsib,
        wz0,
        wzs0,
        gains[1],
        w,
        qk_gain[1],
        ci_own,
        ci_par,
    )
    so, sp, sctx = spread(fo, fp)
    go = attend(0, sc, fo[0], fp[1][1], so, sctx)
    gp = attend(1, sc, fp[0], fo[1][1], sp, sctx)
    atts = [go[0], send(go[1], to_sib), send(gp[0], to_z), send(gp[1], to_diag)]
    return final(sc, atts, others, x0, first, w_out, wsib, wz1, wzs1)


def solution(mesh):
    in_specs = (
        P(("clip", "head"), None),
        P(),
        P(None, None, None, "head"),
        P(),
        P(None, "head", None),
        P("clip"),
        P("clip"),
        P("clip", None),
    )
    out_specs = P(("clip", "head"), None)
    return jax.shard_map(body, mesh=mesh, in_specs=in_specs, out_specs=out_specs, check_vma=False)
```

```python
import functools
import math

import jax
import jax.numpy as jnp
from jax import lax
from jax.experimental import pallas as pl
from jax.experimental.pallas import tpu as pltpu
from jax.sharding import PartitionSpec as P

D = 3072
HD = 128
HL = 3
INNER = HL * HD
BLK = 128
CLIP_TOK = 256
CTX = 8
HALO = 32
QUART = D // 4
GUIDE = 1.5
EPS = 1e-06
AXES = ("clip", "head")
F32, BF16 = jnp.float32, jnp.bfloat16
ANY = pl.BlockSpec(memory_space=pl.ANY)
VM = pl.BlockSpec(memory_space=pltpu.VMEM)
SM = pl.BlockSpec(memory_space=pltpu.SMEM)


def moved(clips, heads, rule):
    pairs = []
    for c in range(clips):
        for h in range(heads):
            to = rule(c, h)
            if to is not None:
                pairs.append((c * heads + h, to[0] * heads + to[1]))
    return pairs


def send(value, rule):
    pairs = moved(lax.axis_size("clip"), lax.axis_size("head"), rule)
    return lax.ppermute(value, AXES, pairs)


def to_sib(c, h):
    return c, h ^ 1


def to_z(c, h):
    return c, h ^ 2


def to_diag(c, h):
    return c, h ^ 3


def to_far(c, h):
    return c ^ 16, h


def to_far_z(c, h):
    return c ^ 16, h ^ 2


def to_x(step):
    return lambda c, h: ((c & ~3) | ((c + step) & 3), h)


def to_y(step):
    return lambda c, h: ((c & ~12) | ((c + 4 * step) & 12), h)


def edge_own(c, h):
    to = c - 1 if h < 2 else c + 1
    return (to, h) if 0 <= to < 32 else None


def edge_par(c, h):
    to = c + 1 if h < 2 else c - 1
    return (to, h) if 0 <= to < 32 else None


def shape(*dims):
    return jax.ShapeDtypeStruct(dims, BF16)


def params(mib):
    return pltpu.CompilerParams(vmem_limit_bytes=mib * 1024 * 1024)


def pack_kernel(*refs):
    out = refs[-1]
    step = out.shape[0] // (len(refs) - 1)
    for i, ref in enumerate(refs[:-1]):
        out[i * step : (i + 1) * step] = ref[...]


def pack(*parts):
    lead, rest = parts[0].shape[0], parts[0].shape[1:]
    return pl.pallas_call(
        pack_kernel,
        out_shape=shape(len(parts) * lead, *rest),
        in_specs=[VM] * len(parts),
        out_specs=VM,
        compiler_params=params(8),
        name="pack",
    )(*parts)


def slot_copies(layer, turn, wo, wsib, wz, wzs, wslot, sems):
    copies = []
    for k in range(4):
        cols = pl.ds(quarter(turn, k), QUART)
        for j, src in enumerate(
            (wo.at[layer, :, cols], wsib.at[layer, :, cols], wz[k], wzs[k])
        ):
            dst = wslot.at[k, pl.ds(j * INNER, INNER)]
            copies.append(pltpu.make_async_copy(src, dst, sems.at[4 * k + j]))
    return copies


def quarter(turn, k):
    off = (0, 3, 1, 2)[k]
    return pl.multiple_of(((turn + off) & 3) * QUART, QUART)


def norm_rows(src, gain, dst, row0, rows):
    def step(i, carry):
        at = pl.ds(pl.multiple_of(i * 16, 16), 16)
        to = pl.ds(pl.multiple_of(row0 + i * 16, 16), 16)
        v = src[at, :].astype(F32)
        ms = jnp.mean(v * v, axis=-1, keepdims=True)
        dst[to, :] = (v * lax.rsqrt(ms + EPS) * gain[...]).astype(BF16)
        return carry

    lax.fori_loop(0, rows // 16, step, 0, unroll=2)


def head_norm(p, gain):
    parts = []
    for h in range(HL):
        ph = p[:, h * HD : (h + 1) * HD]
        ms = jnp.mean(ph * ph, axis=-1, keepdims=True)
        parts.append(ph * lax.rsqrt(ms + EPS) * gain)
    return jnp.concatenate(parts, axis=1)


def weight_copies(w, l, wcat, sems):
    return [
        pltpu.make_async_copy(
            w.at[l, c], wcat.at[:, pl.ds(c * INNER, INNER)], sems.at[c]
        )
        for c in range(3)
    ]


def project(normed, wcat, l, qkg, put, rows):
    def step(m, carry):
        row = pl.multiple_of(m * CLIP_TOK, CLIP_TOK)
        p = jnp.dot(
            normed[pl.ds(row, CLIP_TOK), :], wcat[...], preferred_element_type=F32
        )
        for c in range(3):
            pc = p[:, c * INNER : (c + 1) * INNER]
            if c < 2:
                pc = head_norm(pc, qkg[l, c : c + 1, :])
            put(m, c, pc.astype(BF16))
        return carry

    lax.fori_loop(0, rows // CLIP_TOK, step, 0)


def parity_of(sc, which):
    return sc[1] if which == 0 else 1 - sc[1]


def put_edges(sc, which, rows, outer, inner):
    core, parity = sc[0], parity_of(sc, which)
    for edge, last in ((outer, parity), (inner, 1 - parity)):
        start = pl.multiple_of((last ^ core) * BLK + last * (BLK - HALO), HALO)
        for kv in range(2):
            edge[kv] = rows(kv, pl.ds(start, HALO))


def rows_kernel(sc, ci, x, out):
    core, zlo = sc[0], sc[1]
    row = lax.broadcasted_iota(jnp.int32, (8, BLK), 0)
    col = lax.broadcasted_iota(jnp.int32, (8, BLK), 1)
    at = jnp.full((8, BLK), -1, jnp.int32)
    for r in range(4):
        at = jnp.where(row == r, ci[zlo, 4 * core + r] - core * BLK, at)
    hot = jnp.where(col == at, 1.0, 0.0).astype(BF16)
    got = jnp.dot(hot, x[...], preferred_element_type=F32)
    out[...] = got[:4].astype(BF16)


def context_rows(sc, ci, x):
    return pl.pallas_call(
        rows_kernel,
        out_shape=shape(4, D),
        in_specs=[SM, SM, VM],
        out_specs=VM,
        compiler_params=params(4),
        name="context_rows",
    )(sc, ci, x)


def context_kernel(c0, c1, c2, c3, gain, w, qkg, out, xs, normed, wbuf, sems):
    copies = [
        pltpu.make_async_copy(
            w.at[l, 1 + kv], wbuf.at[2 * l + kv], sems.at[2 * l + kv]
        )
        for l in range(2)
        for kv in range(2)
    ]
    for copy in copies:
        copy.start()
    for j, c in enumerate((c0, c1, c2, c3)):
        xs[4 * j : 4 * j + 4, :] = c[...].astype(F32)
    v = xs[...]
    v = v * lax.rsqrt(jnp.mean(v * v, axis=-1, keepdims=True) + EPS)
    for l in range(2):
        normed[...] = (v * gain[l : l + 1, :]).astype(BF16)
        for kv in range(2):
            copies[2 * l + kv].wait()
            p = jnp.dot(normed[...], wbuf[2 * l + kv], preferred_element_type=F32)
            p = head_norm(p, qkg[l, 1:2, :]) if kv == 0 else p
            out[0, l, kv] = p.astype(BF16)


def context_kv(c, gain, w, qkg):
    return pl.pallas_call(
        context_kernel,
        out_shape=shape(1, 2, 2, 2 * CTX, INNER),
        in_specs=[VM] * 5 + [ANY, VM],
        out_specs=VM,
        scratch_shapes=[
            pltpu.VMEM((2 * CTX, D), F32),
            pltpu.VMEM((2 * CTX, D), BF16),
            pltpu.VMEM((4, D, INNER), BF16),
            pltpu.SemaphoreType.DMA((4,)),
        ],
        compiler_params=params(16),
        cost_estimate=pl.CostEstimate(
            flops=2 * 256 * D * 4 * INNER, transcendentals=0, bytes_accessed=8 * D * INNER
        ),
        name="context_kv",
    )(*c, gain, w, qkg)


def qkv_kernel(
    l, which, sc, xa, xb, gain, w, qkg, out, outer, inner, normed, wcat, sems
):
    copies = weight_copies(w, l, wcat, sems)
    for copy in copies:
        copy.start()
    for k, src in enumerate((xa, xb)):
        norm_rows(src, gain.at[l : l + 1], normed, k * BLK, BLK)
    for copy in copies:
        copy.wait()

    def put(m, c, p):
        out[c] = p

    project(normed, wcat, l, qkg, put, CLIP_TOK)
    put_edges(sc, which, lambda kv, at: out[1 + kv, at, :], outer, inner)


def qkv(l, which, sc, xa, xb, gain, w, qkg):
    return pl.pallas_call(
        functools.partial(qkv_kernel, l, which),
        out_shape=(
            shape(3, CLIP_TOK, INNER),
            shape(2, HALO, INNER),
            shape(2, HALO, INNER),
        ),
        in_specs=[SM] + [VM] * 3 + [ANY, VM],
        out_specs=(VM, VM, VM),
        scratch_shapes=[
            pltpu.VMEM((CLIP_TOK, D), BF16),
            pltpu.VMEM((D, 3 * INNER), BF16),
            pltpu.SemaphoreType.DMA((3,)),
        ],
        compiler_params=params(18),
        cost_estimate=pl.CostEstimate(
            flops=2 * CLIP_TOK * D * 3 * INNER,
            transcendentals=0,
            bytes_accessed=2 * (3 * D * INNER + CLIP_TOK * D),
        ),
        name="qkv",
    )(sc, xa, xb, gain, w, qkg)


def halo_mask(sc, which):
    parity = parity_of(sc, which)
    seen, exists = sc[2 + which], sc[4 + which]
    lane = lax.broadcasted_iota(jnp.int32, (1, 2 * HALO), 1)
    mask = jnp.zeros((1, 2 * HALO), F32)
    for side, count in enumerate((seen, seen * exists)):
        prev = parity if side == 0 else 1 - parity
        low = side * HALO + prev * (HALO - 16 * count)
        mask = jnp.where(lane >= low, jnp.where(lane < low + 16 * count, 1.0, mask), mask)
    return mask


def attend_clip(cl, mask, mine, inner, outer, ctx, put):
    factor = math.log2(math.e) / math.sqrt(HD)
    tn = (((1,), (1,)), ((), ()))

    def step(h, carry):
        cols = pl.ds(pl.multiple_of(h * HD, HD), HD)
        q = mine[0, :, cols]
        rows = []
        for kv in range(2):
            parts = [mine[1 + kv, :, cols]]
            for ref in ctx:
                parts.append(ref[:, cl, kv, :, cols].reshape(-1, HD))
            rows.append(jnp.concatenate(parts, axis=0))
        k, v = rows
        kh = jnp.concatenate([inner[0, :, cols], outer[0, :, cols]], axis=0)
        vh = jnp.concatenate([inner[1, :, cols], outer[1, :, cols]], axis=0)
        v = jnp.concatenate([v, jnp.ones_like(v)], axis=1)
        vh = jnp.concatenate([vh, jnp.ones_like(vh)], axis=1)
        s = lax.dot_general(q, k, tn, preferred_element_type=F32)
        sh = lax.dot_general(q, kh, tn, preferred_element_type=F32)
        p = jnp.exp2(s * factor).astype(BF16)
        ph = (jnp.exp2(sh * factor) * mask).astype(BF16)
        r = jnp.dot(p, v, preferred_element_type=F32)
        r = r + jnp.dot(ph, vh, preferred_element_type=F32)
        put(cols, (r[:, :HD] / r[:, HD:]).astype(BF16))
        return carry

    lax.fori_loop(0, HL, step, 0)


def attend_cost(clips, ctx):
    keys = CLIP_TOK + 2 * HALO + sum(c.shape[0] * c.shape[3] for c in ctx)
    return pl.CostEstimate(
        flops=clips * 6 * CLIP_TOK * keys * INNER,
        transcendentals=clips * HL * CLIP_TOK * keys,
        bytes_accessed=4 * keys * INNER + clips * 4 * CLIP_TOK * INNER,
    )


def attend_kernel(cl, which, sc, mine, inner, outer, c0, c1, c2, c3, out):
    def put(cols, a):
        out[0, :, cols] = a[:BLK]
        out[1, :, cols] = a[BLK:]

    ctx = (c0, c1, c2, c3)
    attend_clip(cl, halo_mask(sc, which), mine, inner, outer, ctx, put)


def attend(cl, which, sc, mine, inner, outer, ctx):
    return pl.pallas_call(
        functools.partial(attend_kernel, cl, which),
        out_shape=shape(2, BLK, INNER),
        in_specs=[SM] + [VM] * 7,
        out_specs=VM,
        compiler_params=params(12),
        cost_estimate=attend_cost(1, ctx),
        name="attend",
    )(sc, mine, inner, outer, *ctx)


def attend_pair_kernel(cl, *refs):
    (sc, qo, io, eo, qp, ip, ep) = refs[:7]
    ctx, (o0, o1, p0, p1) = refs[7:11], refs[11:]
    for which, args, (low, high) in (
        (0, (qo, ip, eo), (o0, o1)),
        (1, (qp, io, ep), (p0, p1)),
    ):

        def put(cols, a, low=low, high=high):
            low[:, cols] = a[:BLK]
            high[:, cols] = a[BLK:]

        attend_clip(cl, halo_mask(sc, which), *args, ctx, put)


def attend_pair(cl, sc, own, par, outer_own, outer_par, ctx):
    return pl.pallas_call(
        functools.partial(attend_pair_kernel, cl),
        out_shape=(shape(BLK, INNER),) * 4,
        in_specs=[SM] + [VM] * 10,
        out_specs=(VM,) * 4,
        compiler_params=params(16),
        cost_estimate=attend_cost(2, ctx),
        name="attend_pair",
    )(sc, own[0], own[2], outer_own, par[0], par[2], outer_par, *ctx)


def first_kernel(*refs):
    (sc, o0, p0, o1, p1, o2, p2, o3, p3, x0, x1, x2, x3, wo, wsib) = refs[:15]
    wz, wzs = refs[15:19], refs[19:23]
    (gain, w, qkg, ci) = refs[23:27]
    (first, qo, eo, io, qp, ep, ip, ctx) = refs[27:35]
    (acat, xbuf, normed, wslot, wcat, wsems, qsems) = refs[35:]
    copies = slot_copies(0, sc[6], wo, wsib, wz, wzs, wslot, wsems)
    late = weight_copies(w, 1, wcat, qsems)
    for copy in copies + late:
        copy.start()
    for j, (ao, ap) in enumerate(((o0, p0), (o1, p1), (p2, o2), (p3, o3))):
        for clip, piece in enumerate((ao, ap)):
            for b in range(2):
                row = (2 * clip + b) * BLK
                acat[row : row + BLK, j * INNER : (j + 1) * INNER] = piece[b ^ (j & 1)]
    rows = 2 * CLIP_TOK
    xs = (x0, x1, x2, x3)
    for k in range(4):
        for copy in copies[4 * k : 4 * k + 4]:
            copy.wait()
        cols = pl.ds(quarter(sc[6], k), QUART)

        def block(m, carry, k=k, cols=cols):
            at = pl.ds(pl.multiple_of(m * CLIP_TOK, CLIP_TOK), CLIP_TOK)
            t = jnp.dot(acat[at, :], wslot[k], preferred_element_type=F32)
            xbuf[at, cols] = t.astype(BF16)
            return carry

        lax.fori_loop(0, 2, block, 0)
    for j in range(4):
        at = slice(j * BLK, (j + 1) * BLK)
        v = xs[j][...].astype(F32) + xbuf[at, :].astype(F32)
        xbuf[at, :] = v.astype(BF16)
    first[...] = xbuf[:BLK, :]
    norm_rows(xbuf, gain.at[1:2], normed, 0, rows)
    for copy in late:
        copy.wait()

    def put(m, c, p):
        @pl.when(m == 0)
        def _():
            qo[c] = p

        @pl.when(m == 1)
        def _():
            qp[c] = p

    project(normed, wcat, 1, qkg, put, rows)
    col = lax.broadcasted_iota(jnp.int32, (CLIP_TOK, CTX), 0)
    found = []
    for which, (q, e, i) in enumerate(((qo, eo, io), (qp, ep, ip))):
        put_edges(sc, which, lambda kv, at, q=q: q[1 + kv, at, :], e, i)
        idx = jnp.where(parity_of(sc, which) == 0, ci[0:1, :], ci[1:2, :])
        rel = ((idx // BLK) ^ sc[0]) * BLK + idx % BLK
        hot = jnp.where(col == rel, 1.0, 0.0).astype(BF16)
        tt = (((0,), (0,)), ((), ()))
        found.append(
            [
                lax.dot_general(hot, q[1 + kv], tt, preferred_element_type=F32)
                for kv in range(2)
            ]
        )
    for kv in range(2):
        both = jnp.concatenate([found[0][kv], found[1][kv]], axis=0)
        ctx[0, 0, kv] = both.astype(BF16)


def first_qkv(sc, atts, xs, wo, wsib, wz, wzs, gain, w, qkg, ci):
    one = (
        shape(3, CLIP_TOK, INNER),
        shape(2, HALO, INNER),
        shape(2, HALO, INNER),
    )
    rows = 2 * CLIP_TOK
    res = pl.pallas_call(
        first_kernel,
        out_shape=(shape(BLK, D),) + one + one + (shape(1, 1, 2, 2 * CTX, INNER),),
        in_specs=[SM] + [VM] * 12 + [ANY] * 10 + [VM, ANY, VM, VM],
        out_specs=(VM,) * 8,
        scratch_shapes=[
            pltpu.VMEM((rows, 4 * INNER), BF16),
            pltpu.VMEM((rows, D), BF16),
            pltpu.VMEM((rows, D), BF16),
            pltpu.VMEM((4, 4 * INNER, QUART), BF16),
            pltpu.VMEM((D, 3 * INNER), BF16),
            pltpu.SemaphoreType.DMA((16,)),
            pltpu.SemaphoreType.DMA((3,)),
        ],
        compiler_params=params(40),
        cost_estimate=pl.CostEstimate(
            flops=2 * rows * D * 7 * INNER,
            transcendentals=0,
            bytes_accessed=2 * (7 * D * INNER + 2 * rows * D),
        ),
        name="first_qkv",
    )(sc, *atts, *xs, wo, wsib, *wz, *wzs, gain, w, qkg, ci)
    return res[0], res[1:4], res[4:7], res[7]


def final_kernel(*refs):
    sc, atts, others = refs[0], refs[1:5], refs[5:9]
    (video, first, wo, wsib) = refs[9:13]
    wz, wzs = refs[13:17], refs[17:21]
    (out, acat, wslot, wsems) = refs[21:]
    copies = slot_copies(1, sc[7], wo, wsib, wz, wzs, wslot, wsems)
    for copy in copies:
        copy.start()
    for j in range(4):
        for b, piece in enumerate((atts[j], others[j])):
            acat[b * BLK : (b + 1) * BLK, j * INNER : (j + 1) * INNER] = piece[...]
    skip_first = sc[8] == 0
    for k in range(4):
        for copy in copies[4 * k : 4 * k + 4]:
            copy.wait()
        cols = pl.ds(quarter(sc[7], k), QUART)
        t = jnp.dot(acat[...], wslot[k], preferred_element_type=F32)
        f = first[:, cols].astype(F32)
        strong = (f + t[:BLK]).astype(BF16).astype(F32)
        other = (video[:, cols].astype(F32) + t[BLK:]).astype(BF16).astype(F32)
        weak = jnp.where(skip_first, other, f)
        out[:, cols] = (strong + GUIDE * (strong - weak)).astype(BF16)


def final(sc, atts, others, video, first, wo, wsib, wz, wzs):
    return pl.pallas_call(
        final_kernel,
        out_shape=shape(BLK, D),
        in_specs=[SM] + [VM] * 10 + [ANY] * 10,
        out_specs=VM,
        scratch_shapes=[
            pltpu.VMEM((2 * BLK, 4 * INNER), BF16),
            pltpu.VMEM((4, 4 * INNER, QUART), BF16),
            pltpu.SemaphoreType.DMA((16,)),
        ],
        compiler_params=params(20),
        cost_estimate=pl.CostEstimate(
            flops=4 * BLK * D * 4 * INNER,
            transcendentals=0,
            bytes_accessed=2 * (4 * D * INNER + 3 * BLK * D),
        ),
        name="final",
    )(sc, *atts, *others, video, first, wo, wsib, *wz, *wzs)


def after(value, *done):
    return lax.optimization_barrier((value,) + done)[0]


def columns(weight, layer, turn):
    mine = lax.dynamic_slice(weight, (layer, 0, turn * QUART), (1, INNER, QUART))
    return mine[0]


def edges(own, par):
    return send(par[1], edge_par), send(own[1], edge_own)


def body(video, norm_gain, w_qkv, qk_gain, w_out, skip_layer, halo_frames, context_index):
    clip = lax.axis_index("clip").astype(jnp.int32)
    head = lax.axis_index("head").astype(jnp.int32)
    clips = lax.axis_size("clip")
    core, zlo = head % 2, head // 2
    not_first = (clip > 0).astype(jnp.int32)
    not_last = (clip < clips - 1).astype(jnp.int32)
    even = zlo == 0
    turn_x, turn_y = clip % 4, clip // 4 % 4
    sc = jnp.stack(
        [
            core,
            zlo,
            jnp.where(even, halo_frames[0], halo_frames[1]),
            jnp.where(even, halo_frames[1], halo_frames[0]),
            jnp.where(even, not_first, not_last),
            jnp.where(even, not_last, not_first),
            turn_x,
            turn_y,
            jnp.where(even, skip_layer[0], skip_layer[1]),
        ]
    ).astype(jnp.int32)
    w = jnp.transpose(w_qkv, (0, 2, 1, 3))

    x0 = video
    c0 = context_rows(sc, context_index, x0)
    c = [c0, send(c0, to_sib), send(c0, to_z), send(c0, to_diag)]
    x2 = send(after(x0, c0), to_z)
    x1 = send(after(x0, c0), to_sib)
    piece0 = columns(w_out, 0, turn_x)
    here0 = send(after(piece0, c0), to_far_z)

    kv = context_kv(c, norm_gain, w, qk_gain)
    kz = send(kv, to_far)
    own0 = qkv(0, 0, sc, after(x0, kv), x1, norm_gain, w, qk_gain)
    kx = pack(kv, after(kz, own0[0]))
    kxs = [send(kx, to_x(d)) for d in (1, 3, 2)]
    own1 = qkv(1, 0, sc, after(x0, kx), x1, norm_gain, w, qk_gain)
    ky = pack(kx, *[after(k, own1[0]) for k in kxs])
    ctx = [ky] + [send(ky, to_y(d)) for d in (1, 3, 2)]
    wz0 = [here0] + [send(after(here0, ky), to_x(d)) for d in (1, 3, 2)]
    piece1 = columns(w_out, 1, turn_y)
    here1 = send(after(piece1, ky), to_far_z)
    wsib = send(after(w_out, ky), to_sib)

    x3 = send(after(x2, ky), to_sib)
    par0 = qkv(0, 1, sc, x2, x3, norm_gain, w, qk_gain)
    eo, ep = edges(own0, par0)
    par1 = qkv(1, 1, sc, after(x2, par0[0]), x3, norm_gain, w, qk_gain)
    wz1 = [here1] + [send(after(here1, par1[0]), to_y(d)) for d in (1, 3, 2)]
    wzs0 = [send(after(p, par1[0]), to_sib) for p in wz0]
    ctx = [ky] + [after(k, par1[0]) for k in ctx[1:]]
    ao = attend(0, 0, sc, own0[0], par0[2], after(eo, par1[0]), ctx)
    oz = send(ao, to_z)
    os = send(ao, to_sib)
    ap = attend(0, 1, sc, after(par0[0], ao), own0[2], ep, ctx)
    pz = send(ap, to_z)
    ps = send(ap, to_sib)
    ozs = send(oz, to_sib)
    pzs = send(pz, to_sib)

    woo, wop = edges(own1, (par1[0], after(par1[1], ap)))
    b = attend_pair(1, sc, (after(own1[0], ap),) + own1[1:], par1, woo, wop, ctx)
    others = [b[0], send(b[1], to_sib), send(b[2], to_z), send(b[3], to_diag)]

    first, fo, fp, fkv = first_qkv(
        sc,
        (ao, ap, os, ps, oz, pz, ozs, pzs),
        (x0, x1, x2, x3),
        w_out,
        wsib,
        wz0,
        wzs0,
        norm_gain,
        after(w, b[0]),
        qk_gain,
        context_index,
    )
    so, sp = edges(fo, fp)
    wzs1 = [send(after(p, fkv), to_sib) for p in wz1]
    fx = pack(fkv, send(fkv, to_far))
    fy = pack(fx, *[send(fx, to_x(d)) for d in (1, 3, 2)])
    fctx = [fy] + [send(fy, to_y(d)) for d in (1, 3, 2)]
    g = attend_pair(0, sc, fo, fp, so, sp, fctx)
    atts = [g[0], send(g[1], to_sib), send(g[2], to_z), send(g[3], to_diag)]
    return final(sc, atts, others, x0, first, w_out, wsib, wz1, wzs1)


def solution(mesh):
    in_specs = (
        P(("clip", "head"), None),
        P(),
        P(None, None, None, "head"),
        P(),
        P(None, "head", None),
        P("clip"),
        P("clip"),
        P("clip", None),
    )
    out_specs = P(("clip", "head"), None)
    return jax.shard_map(body, mesh=mesh, in_specs=in_specs, out_specs=out_specs, check_vma=False)
```

```python
import functools
import math

import jax
import jax.numpy as jnp
from jax import lax
from jax.experimental import pallas as pl
from jax.experimental.pallas import tpu as pltpu
from jax.sharding import PartitionSpec as P


D = 3072
HD = 128
HL = 3
INNER = HL * HD
BLK = 128
CLIP_TOK = 256
CTX = 8
HALO = 32
QUART = D // 4
GUIDE = 1.5
EPS = 1e-06
AXES = ("clip", "head")
F32, BF16 = jnp.float32, jnp.bfloat16
ANY = pl.BlockSpec(memory_space=pl.ANY)
VM = pl.BlockSpec(memory_space=pltpu.VMEM)
SM = pl.BlockSpec(memory_space=pltpu.SMEM)


def moved(clips, heads, rule):
    pairs = []
    for c in range(clips):
        for h in range(heads):
            to = rule(c, h)
            if to is not None:
                pairs.append((c * heads + h, to[0] * heads + to[1]))
    return pairs


def send(value, rule):
    pairs = moved(lax.axis_size("clip"), lax.axis_size("head"), rule)
    return lax.ppermute(value, AXES, pairs)


def to_sib(c, h):
    return c, h ^ 1


def to_z(c, h):
    return c, h ^ 2


def to_diag(c, h):
    return c, h ^ 3


def to_far(c, h):
    return c ^ 16, h


def to_far_z(c, h):
    return c ^ 16, h ^ 2


def to_x(step):
    return lambda c, h: ((c & ~3) | ((c + step) & 3), h)


def to_y(step):
    return lambda c, h: ((c & ~12) | ((c + 4 * step) & 12), h)


def edge_own(c, h):
    to = c - 1 if h < 2 else c + 1
    return (to, h) if 0 <= to < 32 else None


def edge_par(c, h):
    to = c + 1 if h < 2 else c - 1
    return (to, h) if 0 <= to < 32 else None


def shape(*dims):
    return jax.ShapeDtypeStruct(dims, BF16)


def params(mib):
    return pltpu.CompilerParams(vmem_limit_bytes=mib * 1024 * 1024)


def pack_kernel(*refs):
    out = refs[-1]
    step = out.shape[0] // (len(refs) - 1)
    for i, ref in enumerate(refs[:-1]):
        out[i * step : (i + 1) * step] = ref[...]


def pack(*parts):
    lead, rest = parts[0].shape[0], parts[0].shape[1:]
    return pl.pallas_call(
        pack_kernel,
        out_shape=shape(len(parts) * lead, *rest),
        in_specs=[VM] * len(parts),
        out_specs=VM,
        compiler_params=params(4),
        name="pack",
    )(*parts)


def quarter(turn, k):
    off = jnp.where(k == 0, 0, jnp.where(k == 1, 3, k - 1))
    return pl.multiple_of(((turn + off) & 3) * QUART, QUART)


def stage_kernel(w, out, sems):
    copies = [
        pltpu.make_async_copy(
            w.at[l, c], out.at[l, :, pl.ds(c * INNER, INNER)], sems.at[3 * l + c]
        )
        for l in range(2)
        for c in range(3)
    ]
    for copy in copies:
        copy.start()
    for copy in copies:
        copy.wait()


def stage(w):
    return pl.pallas_call(
        stage_kernel,
        out_shape=pltpu.VMEM((2, D, 3 * INNER), BF16),
        in_specs=[pl.BlockSpec(memory_space=pltpu.HBM)],
        out_specs=VM,
        scratch_shapes=[pltpu.SemaphoreType.DMA((6,))],
        compiler_params=params(2),
        name="stage",
    )(w)


def assemble_kernel(layer, wo, wsib, *refs):
    wz, wzs, out, sems = refs[:4], refs[4:8], refs[8], refs[9]
    copies = []
    for k in range(4):
        cols = pl.ds(quarter(place()[2 + layer], k), QUART)
        for j, src in enumerate(
            (wo.at[layer, :, cols], wsib.at[layer, :, cols], wz[k], wzs[k])
        ):
            dst = out.at[k, pl.ds(j * INNER, INNER)]
            copies.append(pltpu.make_async_copy(src, dst, sems.at[4 * k + j]))
    for copy in copies:
        copy.start()
    for copy in copies:
        copy.wait()


def assemble(layer, wo, wsib, wz, wzs):
    hbm = pl.BlockSpec(memory_space=pltpu.HBM)
    return pl.pallas_call(
        functools.partial(assemble_kernel, layer),
        out_shape=pltpu.VMEM((4, 4 * INNER, QUART), BF16),
        in_specs=[hbm] * 10,
        out_specs=VM,
        scratch_shapes=[pltpu.SemaphoreType.DMA((16,))],
        compiler_params=params(2),
        name="assemble",
    )(wo, wsib, *wz, *wzs)


def norm_rows(src, gain, dst, row0, rows):
    def step(i, carry):
        at = pl.ds(pl.multiple_of(i * 16, 16), 16)
        to = pl.ds(pl.multiple_of(row0 + i * 16, 16), 16)
        v = src[at, :].astype(F32)
        ms = jnp.mean(v * v, axis=-1, keepdims=True)
        dst[to, :] = (v * lax.rsqrt(ms + EPS) * gain[...]).astype(BF16)
        return carry

    lax.fori_loop(0, rows // 16, step, 0)


def head_norm(p, gain):
    parts = []
    for h in range(HL):
        ph = p[:, h * HD : (h + 1) * HD]
        ms = jnp.mean(ph * ph, axis=-1, keepdims=True)
        parts.append(ph * lax.rsqrt(ms + EPS) * gain)
    return jnp.concatenate(parts, axis=1)


def project(normed, w, l, qkg, put, rows):
    def step(m, carry):
        row = pl.multiple_of(m * CLIP_TOK, CLIP_TOK)
        p = jnp.dot(
            normed[pl.ds(row, CLIP_TOK), :], w[l], preferred_element_type=F32
        )
        for c in range(3):
            pc = p[:, c * INNER : (c + 1) * INNER]
            if c < 2:
                pc = head_norm(pc, qkg[l, c : c + 1, :])
            put(m, c, pc.astype(BF16))
        return carry

    lax.fori_loop(0, rows // CLIP_TOK, step, 0)


def place():
    clip, head = lax.axis_index("clip"), lax.axis_index("head")
    return head & 1, head >> 1, clip & 3, (clip >> 2) & 3


def parity_of(which):
    zlo = place()[1]
    return zlo if which == 0 else 1 - zlo


def put_edges(which, rows, outer, inner):
    core, parity = place()[0], parity_of(which)
    for edge, last in ((outer, parity), (inner, 1 - parity)):
        start = pl.multiple_of((last ^ core) * BLK + last * (BLK - HALO), HALO)
        for kv in range(2):
            edge[kv] = rows(kv, pl.ds(start, HALO))


def rows_kernel(ci, x, out, low, high):
    low[...] = x[: BLK // 2, :]
    high[...] = x[BLK // 2 :, :]
    core, zlo = place()[:2]
    row = lax.broadcasted_iota(jnp.int32, (8, BLK), 0)
    col = lax.broadcasted_iota(jnp.int32, (8, BLK), 1)
    at = jnp.full((8, BLK), -1, jnp.int32)
    for r in range(4):
        at = jnp.where(row == r, ci[zlo, 4 * core + r] - core * BLK, at)
    hot = jnp.where(col == at, 1.0, 0.0).astype(BF16)
    got = jnp.dot(hot, x[...], preferred_element_type=F32)
    out[...] = got[:4].astype(BF16)


def context_rows(ci, x):
    return pl.pallas_call(
        rows_kernel,
        out_shape=(shape(4, D), shape(BLK // 2, D), shape(BLK // 2, D)),
        in_specs=[SM, VM],
        out_specs=(VM, VM, VM),
        compiler_params=params(4),
        name="context_rows",
    )(ci, x)


def context_kernel(c0, c1, c2, c3, gain, w, qkg, out, xs, normed):
    for j, c in enumerate((c0, c1, c2, c3)):
        xs[4 * j : 4 * j + 4, :] = c[...].astype(F32)
    v = xs[...]
    v = v * lax.rsqrt(jnp.mean(v * v, axis=-1, keepdims=True) + EPS)
    xs[...] = v

    def step(l, carry):
        normed[...] = (xs[...] * gain[pl.ds(l, 1), :]).astype(BF16)
        p = jnp.dot(normed[...], w[l, :, INNER:], preferred_element_type=F32)
        out[0, l, 0] = head_norm(p[:, :INNER], qkg[l, 1:2, :]).astype(BF16)
        out[0, l, 1] = p[:, INNER:].astype(BF16)
        return carry

    lax.fori_loop(0, 2, step, 0)


def context_kv(c, gain, w, qkg):
    return pl.pallas_call(
        context_kernel,
        out_shape=shape(1, 2, 2, 2 * CTX, INNER),
        in_specs=[VM] * 7,
        out_specs=VM,
        scratch_shapes=[
            pltpu.VMEM((2 * CTX, D), F32),
            pltpu.VMEM((2 * CTX, D), BF16),
        ],
        compiler_params=params(4),
        cost_estimate=pl.CostEstimate(
            flops=2 * 256 * D * 4 * INNER, transcendentals=0, bytes_accessed=8 * D * INNER
        ),
        name="context_kv",
    )(*c, gain, w, qkg)


def qkv_kernel(l, which, *refs):
    pieces, (gain, w, qkg, out, outer, inner, normed) = refs[:-7], refs[-7:]
    row = 0
    for src in pieces:
        norm_rows(src, gain.at[l : l + 1], normed, row, src.shape[0])
        row += src.shape[0]

    def put(m, c, p):
        out[c] = p

    project(normed, w, l, qkg, put, CLIP_TOK)
    put_edges(which, lambda kv, at: out[1 + kv, at, :], outer, inner)


def qkv(l, which, pieces, gain, w, qkg):
    return pl.pallas_call(
        functools.partial(qkv_kernel, l, which),
        out_shape=(
            shape(3, CLIP_TOK, INNER),
            shape(2, HALO, INNER),
            shape(2, HALO, INNER),
        ),
        in_specs=[VM] * (len(pieces) + 3),
        out_specs=(VM, VM, VM),
        scratch_shapes=[pltpu.VMEM((CLIP_TOK, D), BF16)],
        compiler_params=params(7),
        cost_estimate=pl.CostEstimate(
            flops=2 * CLIP_TOK * D * 3 * INNER,
            transcendentals=0,
            bytes_accessed=2 * (3 * D * INNER + CLIP_TOK * D),
        ),
        name="qkv",
    )(*pieces, gain, w, qkg)


def halo_mask(halo, which):
    parity = parity_of(which)
    seen = halo[parity]
    end = jnp.where(parity == 0, 0, lax.axis_size("clip") - 1)
    exists = jnp.where(lax.axis_index("clip") == end, 0, 1)
    lane = lax.broadcasted_iota(jnp.int32, (1, 2 * HALO), 1)
    mask = jnp.zeros((1, 2 * HALO), F32)
    for side, count in enumerate((seen, seen * exists)):
        prev = parity if side == 0 else 1 - parity
        low = side * HALO + prev * (HALO - 16 * count)
        mask = jnp.where(lane >= low, jnp.where(lane < low + 16 * count, 1.0, mask), mask)
    return mask


def attend_clip(cl, mask, mine, inner, outer, ctx, put, at=0):
    factor = math.log2(math.e) / math.sqrt(HD)
    tn = (((1,), (1,)), ((), ()))

    def step(h, carry):
        cols = pl.ds(pl.multiple_of(h * HD, HD), HD)
        q = mine[0, :, cols]
        rows = []
        for kv in range(2):
            parts = [mine[1 + kv, :, cols]]
            for ref in ctx:
                parts.append(ref[:, cl, kv, :, cols].reshape(-1, HD))
            rows.append(jnp.concatenate(parts, axis=0))
        k, v = rows
        kh = jnp.concatenate([inner[0, :, cols], outer[at, :, cols]], axis=0)
        vh = jnp.concatenate([inner[1, :, cols], outer[at + 1, :, cols]], axis=0)
        v = jnp.concatenate([v, jnp.ones_like(v)], axis=1)
        vh = jnp.concatenate([vh, jnp.ones_like(vh)], axis=1)
        s = lax.dot_general(q, k, tn, preferred_element_type=F32)
        sh = lax.dot_general(q, kh, tn, preferred_element_type=F32)
        p = jnp.exp2(s * factor).astype(BF16)
        ph = (jnp.exp2(sh * factor) * mask).astype(BF16)
        r = jnp.dot(p, v, preferred_element_type=F32)
        r = r + jnp.dot(ph, vh, preferred_element_type=F32)
        put(cols, (r[:, :HD] / r[:, HD:]).astype(BF16))
        return carry

    lax.fori_loop(0, HL, step, 0)


def attend_cost(clips, ctx):
    keys = CLIP_TOK + 2 * HALO + sum(c.shape[0] * c.shape[3] for c in ctx)
    return pl.CostEstimate(
        flops=clips * 6 * CLIP_TOK * keys * INNER,
        transcendentals=clips * HL * CLIP_TOK * keys,
        bytes_accessed=4 * keys * INNER + clips * 4 * CLIP_TOK * INNER,
    )


def attend_kernel(cl, which, halo, mine, inner, outer, c0, c1, c2, c3, out):
    def put(cols, a):
        out[0, :, cols] = a[:BLK]
        out[1, :, cols] = a[BLK:]

    ctx = (c0, c1, c2, c3)
    attend_clip(cl, halo_mask(halo, which), mine, inner, outer, ctx, put)


def attend(cl, which, halo, mine, inner, outer, ctx):
    return pl.pallas_call(
        functools.partial(attend_kernel, cl, which),
        out_shape=shape(2, BLK, INNER),
        in_specs=[SM] + [VM] * 7,
        out_specs=VM,
        compiler_params=params(7),
        cost_estimate=attend_cost(1, ctx),
        name="attend",
    )(halo, mine, inner, outer, *ctx)


def attend_pair_kernel(cl, at, *refs):
    (halo, qo, io, eo, qp, ip, ep) = refs[:7]
    ctx, (o0, o1, p0, p1) = refs[7:11], refs[11:]
    for which, args, (low, high) in (
        (0, (qo, ip, eo), (o0, o1)),
        (1, (qp, io, ep), (p0, p1)),
    ):

        def put(cols, a, low=low, high=high):
            low[:, cols] = a[:BLK]
            high[:, cols] = a[BLK:]

        attend_clip(cl, halo_mask(halo, which), *args, ctx, put, at)


def attend_pair(cl, at, halo, own, par, outer_own, outer_par, ctx):
    return pl.pallas_call(
        functools.partial(attend_pair_kernel, cl, at),
        out_shape=(shape(BLK, INNER),) * 4,
        in_specs=[SM] + [VM] * 10,
        out_specs=(VM,) * 4,
        compiler_params=params(7),
        cost_estimate=attend_cost(2, ctx),
        name="attend_pair",
    )(halo, own[0], own[2], outer_own, par[0], par[2], outer_par, *ctx)


def first_kernel(*refs):
    (o0, p0, o1, p1, o2, p2, o3, p3) = refs[:8]
    xs, refs = refs[8:-16], refs[-16:]
    (wslot, gain, w, qkg, ci) = refs[:5]
    (first, qo, eo, io, qp, ep, ip, ctx) = refs[5:13]
    (acat, xbuf, normed) = refs[13:]
    for j, (ao, ap) in enumerate(((o0, p0), (o1, p1), (p2, o2), (p3, o3))):
        for clip, piece in enumerate((ao, ap)):
            for b in range(2):
                row = (2 * clip + b) * BLK
                acat[row : row + BLK, j * INNER : (j + 1) * INNER] = piece[b ^ (j & 1)]
    rows = 2 * CLIP_TOK

    def block(k, carry):
        cols = pl.ds(quarter(place()[2], k), QUART)
        row = 0
        for x in xs:
            if row % CLIP_TOK == 0:
                left = acat[row : row + CLIP_TOK, :]
                t = jnp.dot(left, wslot[k], preferred_element_type=F32)
            end = row + x.shape[0]
            base = row - row % CLIP_TOK
            v = x[:, cols].astype(F32) + t[row - base : end - base]
            xbuf[row:end, cols] = v.astype(BF16)
            row = end
        return carry

    lax.fori_loop(0, 4, block, 0)
    first[...] = xbuf[:BLK, :]
    norm_rows(xbuf, gain.at[1:2], normed, 0, rows)

    def put(m, c, p):
        @pl.when(m == 0)
        def _():
            qo[c] = p

        @pl.when(m == 1)
        def _():
            qp[c] = p

    project(normed, w, 1, qkg, put, rows)
    col = lax.broadcasted_iota(jnp.int32, (CLIP_TOK, CTX), 0)
    found = []
    for which, (q, e, i) in enumerate(((qo, eo, io), (qp, ep, ip))):
        put_edges(which, lambda kv, at, q=q: q[1 + kv, at, :], e, i)
        idx = jnp.where(parity_of(which) == 0, ci[0:1, :], ci[1:2, :])
        rel = ((idx // BLK) ^ place()[0]) * BLK + idx % BLK
        hot = jnp.where(col == rel, 1.0, 0.0).astype(BF16)
        tt = (((0,), (0,)), ((), ()))
        found.append(
            [
                lax.dot_general(hot, q[1 + kv], tt, preferred_element_type=F32)
                for kv in range(2)
            ]
        )
    for kv in range(2):
        both = jnp.concatenate([found[0][kv], found[1][kv]], axis=0)
        ctx[0, 0, kv] = both.astype(BF16)


def first_qkv(atts, xs, wslot, gain, w, qkg, ci):
    one = (
        shape(3, CLIP_TOK, INNER),
        shape(2, HALO, INNER),
        shape(2, HALO, INNER),
    )
    rows = 2 * CLIP_TOK
    res = pl.pallas_call(
        first_kernel,
        out_shape=(shape(BLK, D),) + one + one + (shape(1, 1, 2, 2 * CTX, INNER),),
        in_specs=[VM] * (13 + len(xs)),
        out_specs=(VM,) * 8,
        scratch_shapes=[
            pltpu.VMEM((rows, 4 * INNER), BF16),
            pltpu.VMEM((rows, D), BF16),
            pltpu.VMEM((rows, D), BF16),
        ],
        compiler_params=params(14),
        cost_estimate=pl.CostEstimate(
            flops=2 * rows * D * 7 * INNER,
            transcendentals=0,
            bytes_accessed=2 * (7 * D * INNER + 2 * rows * D),
        ),
        name="first_qkv",
    )(*atts, *xs, wslot, gain, w, qkg, ci)
    return res[0], res[1:4], res[4:7], res[7]


def final_kernel(*refs):
    skip, atts, others = refs[0], refs[1:5], refs[5:9]
    (video, first, wslot, out, acat) = refs[9:]
    for j in range(4):
        for b, piece in enumerate((atts[j], others[j])):
            acat[b * BLK : (b + 1) * BLK, j * INNER : (j + 1) * INNER] = piece[...]
    skip_first = skip[place()[1]] == 0

    def block(k, carry):
        cols = pl.ds(quarter(place()[3], k), QUART)
        t = jnp.dot(acat[...], wslot[k], preferred_element_type=F32)
        f = first[:, cols].astype(F32)
        strong = (f + t[:BLK]).astype(BF16).astype(F32)
        other = (video[:, cols].astype(F32) + t[BLK:]).astype(BF16).astype(F32)
        weak = jnp.where(skip_first, other, f)
        out[:, cols] = (strong + GUIDE * (strong - weak)).astype(BF16)
        return carry

    lax.fori_loop(0, 4, block, 0)


def final(skip, atts, others, video, first, wslot):
    return pl.pallas_call(
        final_kernel,
        out_shape=shape(BLK, D),
        in_specs=[SM] + [VM] * 11,
        out_specs=VM,
        scratch_shapes=[pltpu.VMEM((2 * BLK, 4 * INNER), BF16)],
        compiler_params=params(7),
        cost_estimate=pl.CostEstimate(
            flops=4 * BLK * D * 4 * INNER,
            transcendentals=0,
            bytes_accessed=2 * (4 * D * INNER + 3 * BLK * D),
        ),
        name="final",
    )(skip, *atts, *others, video, first, wslot)


def after(value, *done):
    return lax.optimization_barrier((value,) + done)[0]


def columns_kernel(wo, *refs):
    outs, sems = refs[:2], refs[2]
    copies = []
    for l in range(2):
        cols = pl.ds(pl.multiple_of(place()[2 + l] * QUART, QUART), QUART)
        copies.append(
            pltpu.make_async_copy(wo.at[l, :, cols], outs[l], sems.at[l])
        )
    for copy in copies:
        copy.start()
    for copy in copies:
        copy.wait()


def columns(weight):
    return pl.pallas_call(
        columns_kernel,
        out_shape=(shape(INNER, QUART),) * 2,
        in_specs=[pl.BlockSpec(memory_space=pltpu.HBM)],
        out_specs=(VM, VM),
        scratch_shapes=[pltpu.SemaphoreType.DMA((2,))],
        compiler_params=params(3),
        name="columns",
    )(weight)


def edges(own, par):
    return send(par[1], edge_par), send(own[1], edge_own)


def body(video, norm_gain, w_qkv, qk_gain, w_out, skip_layer, halo_frames, context_index):
    x0 = video
    piece0, piece1 = columns(w_out)
    here0 = send(piece0, to_far_z)
    c0, xa, xb = context_rows(context_index, after(x0, piece0))
    c = [c0, send(c0, to_sib), send(c0, to_z), send(c0, to_diag)]
    x2a = send(xa, to_z)
    x1 = send(after(x0, c0), to_sib)
    w = stage(jnp.transpose(w_qkv, (0, 2, 1, 3)))
    kv = context_kv(c, norm_gain, w, qk_gain)
    kz = send(kv, to_far)
    x2b = send(after(xb, kv), to_z)
    own0 = qkv(0, 0, (after(x0, kv), x1), norm_gain, w, qk_gain)
    kx = pack(kv, after(kz, own0[0]))
    kxs = [send(kx, to_x(d)) for d in (1, 3, 2)]
    wz0 = [here0] + [send(after(here0, kx), to_x(d)) for d in (1, 3, 2)]
    x3a = send(after(x2a, kx), to_sib)
    own1 = qkv(1, 0, (after(x0, kx), x1), norm_gain, w, qk_gain)
    ky = pack(kx, *[after(k, own1[0]) for k in kxs])
    kys = [send(ky, to_y(d)) for d in (1, 3, 2)]
    x3b = send(after(x2b, own1[0]), to_sib)
    halves = (after(x2a, ky), x2b, x3a, x3b)
    par0 = qkv(0, 1, halves, norm_gain, w, qk_gain)
    eo, ep = edges(own0, par0)
    wsib = send(after(w_out, par0[0]), to_sib)
    here1 = send(after(piece1, par0[0]), to_far_z)
    ctx = [ky] + kys
    ao = attend(0, 0, halo_frames, own0[0], par0[2], eo, ctx)
    oz = send(ao, to_z)
    os = send(ao, to_sib)
    ap = attend(0, 1, halo_frames, after(par0[0], ao), own0[2], ep, ctx)
    pz = send(ap, to_z)
    ps = send(ap, to_sib)
    halves = (after(x2a, ap), x2b, x3a, x3b)
    par1 = qkv(1, 1, halves, norm_gain, w, qk_gain)
    wzs0 = [send(after(p, ap), to_sib) for p in wz0]
    wz1 = [here1] + [send(after(here1, par1[0]), to_y(d)) for d in (1, 3, 2)]
    ozs = send(after(oz, par1[0]), to_sib)
    wslot0 = assemble(0, after(w_out, par1[0]), wsib, wz0, wzs0)
    pzs = send(pz, to_sib)

    first, fo, fp, fkv = first_qkv(
        (ao, ap, os, ps, oz, pz, ozs, pzs),
        (x0, x1, x2a, x2b, x3a, x3b),
        wslot0,
        norm_gain,
        w,
        qk_gain,
        context_index,
    )
    fz = send(fkv, to_far)
    both_own = pack(own1[1], fo[1])
    both_par = pack(par1[1], fp[1])
    fx = pack(fkv, fz)
    fxs = [send(fx, to_x(d)) for d in (1, 3, 2)]
    so, sp = edges((None, after(both_own, fx)), (None, after(both_par, fx)))
    fy = pack(fx, *fxs)
    fys = [send(fy, to_y(d)) for d in (1, 3, 2)]
    mine = (after(own1[0], fy),) + own1[1:]
    b = attend_pair(1, 0, halo_frames, mine, par1, so, sp, ctx)
    others = [b[0], send(b[1], to_sib), send(b[2], to_z), send(b[3], to_diag)]
    mine = (after(fo[0], b[0]),) + fo[1:]
    g = attend_pair(0, 2, halo_frames, mine, fp, so, sp, [fy] + fys)
    atts = [g[0], send(g[1], to_sib), send(g[2], to_z), send(g[3], to_diag)]
    wzs1 = [send(after(p, b[0]), to_sib) for p in wz1]
    wslot1 = assemble(1, after(w_out, g[0]), wsib, wz1, wzs1)
    return final(skip_layer, atts, others, x0, first, wslot1)


def solution(mesh):
    in_specs = (
        P(("clip", "head"), None),
        P(),
        P(None, None, None, "head"),
        P(),
        P(None, "head", None),
        P("clip"),
        P("clip"),
        P("clip", None),
    )
    out_specs = P(("clip", "head"), None)

    return jax.shard_map(
        body, mesh=mesh, in_specs=in_specs, out_specs=out_specs, check_vma=False
    )
```

```python
import functools
import math

import jax
import jax.numpy as jnp
from jax import lax
from jax.experimental import pallas as pl
from jax.experimental.pallas import tpu as pltpu
from jax.sharding import PartitionSpec as P


D = 3072
HD = 128
HL = 3
INNER = HL * HD
BLK = 128
CLIP_TOK = 256
CTX = 8
HALO = 32
QUART = D // 4
GUIDE = 1.5
EPS = 1e-06
AXES = ("clip", "head")
F32, BF16 = jnp.float32, jnp.bfloat16
ANY = pl.BlockSpec(memory_space=pl.ANY)
VM = pl.BlockSpec(memory_space=pltpu.VMEM)
SM = pl.BlockSpec(memory_space=pltpu.SMEM)


def moved(clips, heads, rule):
    pairs = []
    for c in range(clips):
        for h in range(heads):
            to = rule(c, h)
            if to is not None:
                pairs.append((c * heads + h, to[0] * heads + to[1]))
    return pairs


def send(value, rule):
    pairs = moved(lax.axis_size("clip"), lax.axis_size("head"), rule)
    return lax.ppermute(value, AXES, pairs)


def to_sib(c, h):
    return c, h ^ 1


def to_z(c, h):
    return c, h ^ 2


def to_diag(c, h):
    return c, h ^ 3


def to_far(c, h):
    return c ^ 16, h


def to_far_z(c, h):
    return c ^ 16, h ^ 2


def to_x(step):
    return lambda c, h: ((c & ~3) | ((c + step) & 3), h)


def to_y(step):
    return lambda c, h: ((c & ~12) | ((c + 4 * step) & 12), h)


def edge_own(c, h):
    to = c - 1 if h < 2 else c + 1
    return (to, h) if 0 <= to < 32 else None


def edge_par(c, h):
    to = c + 1 if h < 2 else c - 1
    return (to, h) if 0 <= to < 32 else None


def shape(*dims):
    return jax.ShapeDtypeStruct(dims, BF16)


def params(mib):
    return pltpu.CompilerParams(vmem_limit_bytes=mib * 1024 * 1024)


def pack_kernel(*refs):
    out = refs[-1]
    step = out.shape[0] // (len(refs) - 1)
    for i, ref in enumerate(refs[:-1]):
        out[i * step : (i + 1) * step] = ref[...]


def pack(*parts):
    lead, rest = parts[0].shape[0], parts[0].shape[1:]
    return pl.pallas_call(
        pack_kernel,
        out_shape=shape(len(parts) * lead, *rest),
        in_specs=[VM] * len(parts),
        out_specs=VM,
        compiler_params=params(4),
        name="pack",
    )(*parts)


def quarter(turn, k):
    off = jnp.where(k == 0, 0, jnp.where(k == 1, 3, k - 1))
    return pl.multiple_of(((turn + off) & 3) * QUART, QUART)


def stage_kernel(w, out, sems):
    copies = [
        pltpu.make_async_copy(
            w.at[l, c], out.at[l, :, pl.ds(c * INNER, INNER)], sems.at[3 * l + c]
        )
        for l in range(2)
        for c in range(3)
    ]
    for copy in copies:
        copy.start()
    for copy in copies:
        copy.wait()


def stage(w):
    return pl.pallas_call(
        stage_kernel,
        out_shape=pltpu.VMEM((2, D, 3 * INNER), BF16),
        in_specs=[pl.BlockSpec(memory_space=pltpu.HBM)],
        out_specs=VM,
        scratch_shapes=[pltpu.SemaphoreType.DMA((6,))],
        compiler_params=params(2),
        name="stage",
    )(w)


def assemble_kernel(layer, wo, wsib, *refs):
    wz, wzs, out, sems = refs[:4], refs[4:8], refs[8], refs[9]
    copies = []
    for k in range(4):
        cols = pl.ds(quarter(place()[3 - layer], k), QUART)
        for j, src in enumerate(
            (wo.at[layer, :, cols], wsib.at[layer, :, cols], wz[k], wzs[k])
        ):
            dst = out.at[k, pl.ds(j * INNER, INNER)]
            copies.append(pltpu.make_async_copy(src, dst, sems.at[4 * k + j]))
    for copy in copies:
        copy.start()
    for copy in copies:
        copy.wait()


def assemble(layer, wo, wsib, wz, wzs):
    hbm = pl.BlockSpec(memory_space=pltpu.HBM)
    return pl.pallas_call(
        functools.partial(assemble_kernel, layer),
        out_shape=pltpu.VMEM((4, 4 * INNER, QUART), BF16),
        in_specs=[hbm] * 10,
        out_specs=VM,
        scratch_shapes=[pltpu.SemaphoreType.DMA((16,))],
        compiler_params=params(2),
        name="assemble",
    )(wo, wsib, *wz, *wzs)


def norm_rows(pieces, gain, dst, unroll=1):
    rows = pieces[0].shape[0]

    def step(i, carry):
        at = pl.ds(pl.multiple_of(i * 16, 16), 16)
        for k, src in enumerate(pieces):
            to = pl.ds(pl.multiple_of(k * rows + i * 16, 16), 16)
            v = src[at, :].astype(F32)
            ms = jnp.mean(v * v, axis=-1, keepdims=True)
            dst[to, :] = (v * lax.rsqrt(ms + EPS) * gain[...]).astype(BF16)
        return carry

    lax.fori_loop(0, rows // 16, step, 0, unroll=unroll)


def head_norm(p, gain):
    parts = []
    for h in range(HL):
        ph = p[:, h * HD : (h + 1) * HD]
        ms = jnp.mean(ph * ph, axis=-1, keepdims=True)
        parts.append(ph * lax.rsqrt(ms + EPS) * gain)
    return jnp.concatenate(parts, axis=1)


def project(normed, w, l, qkg, put, rows):
    def step(m, carry):
        row = pl.multiple_of(m * CLIP_TOK, CLIP_TOK)
        p = jnp.dot(
            normed[pl.ds(row, CLIP_TOK), :], w[l], preferred_element_type=F32
        )
        for c in range(3):
            pc = p[:, c * INNER : (c + 1) * INNER]
            if c < 2:
                pc = head_norm(pc, qkg[l, c : c + 1, :])
            put(m, c, pc.astype(BF16))
        return carry

    lax.fori_loop(0, rows // CLIP_TOK, step, 0)


def place():
    clip, head = lax.axis_index("clip"), lax.axis_index("head")
    return head & 1, head >> 1, clip & 3, (clip >> 2) & 3


def parity_of(which):
    zlo = place()[1]
    return zlo if which == 0 else 1 - zlo


def put_edges(which, rows, outer, inner):
    core, parity = place()[0], parity_of(which)
    for edge, last in ((outer, parity), (inner, 1 - parity)):
        start = pl.multiple_of((last ^ core) * BLK + last * (BLK - HALO), HALO)
        for kv in range(2):
            edge[kv] = rows(kv, pl.ds(start, HALO))


def rows_kernel(ci, x, out, low, high):
    low[...] = x[: BLK // 2, :]
    high[...] = x[BLK // 2 :, :]
    core, zlo = place()[:2]
    row = lax.broadcasted_iota(jnp.int32, (8, BLK), 0)
    col = lax.broadcasted_iota(jnp.int32, (8, BLK), 1)
    at = jnp.full((8, BLK), -1, jnp.int32)
    for r in range(4):
        at = jnp.where(row == r, ci[zlo, 4 * core + r] - core * BLK, at)
    hot = jnp.where(col == at, 1.0, 0.0).astype(BF16)
    got = jnp.dot(hot, x[...], preferred_element_type=F32)
    out[...] = got[:4].astype(BF16)


def context_rows(ci, x):
    return pl.pallas_call(
        rows_kernel,
        out_shape=(shape(4, D), shape(BLK // 2, D), shape(BLK // 2, D)),
        in_specs=[SM, VM],
        out_specs=(VM, VM, VM),
        compiler_params=params(4),
        name="context_rows",
    )(ci, x)


def context_kernel(c0, c1, c2, c3, gain, w, qkg, out, xs, normed):
    for j, c in enumerate((c0, c1, c2, c3)):
        xs[4 * j : 4 * j + 4, :] = c[...].astype(F32)
    v = xs[...]
    v = v * lax.rsqrt(jnp.mean(v * v, axis=-1, keepdims=True) + EPS)
    xs[...] = v

    def step(l, carry):
        normed[...] = (xs[...] * gain[pl.ds(l, 1), :]).astype(BF16)
        p = jnp.dot(normed[...], w[l, :, INNER:], preferred_element_type=F32)
        out[0, l, 0] = head_norm(p[:, :INNER], qkg[l, 1:2, :]).astype(BF16)
        out[0, l, 1] = p[:, INNER:].astype(BF16)
        return carry

    lax.fori_loop(0, 2, step, 0)


def context_kv(c, gain, w, qkg):
    return pl.pallas_call(
        context_kernel,
        out_shape=shape(1, 2, 2, 2 * CTX, INNER),
        in_specs=[VM] * 7,
        out_specs=VM,
        scratch_shapes=[
            pltpu.VMEM((2 * CTX, D), F32),
            pltpu.VMEM((2 * CTX, D), BF16),
        ],
        compiler_params=params(4),
        cost_estimate=pl.CostEstimate(
            flops=2 * 256 * D * 4 * INNER, transcendentals=0, bytes_accessed=8 * D * INNER
        ),
        name="context_kv",
    )(*c, gain, w, qkg)


def qkv_kernel(l, which, *refs):
    pieces, (gain, w, qkg, out, outer, inner, normed) = refs[:-7], refs[-7:]
    norm_rows(pieces, gain.at[l : l + 1], normed, 4 // len(pieces))

    def put(m, c, p):
        out[c] = p

    project(normed, w, l, qkg, put, CLIP_TOK)
    put_edges(which, lambda kv, at: out[1 + kv, at, :], outer, inner)


def qkv(l, which, pieces, gain, w, qkg):
    return pl.pallas_call(
        functools.partial(qkv_kernel, l, which),
        out_shape=(
            shape(3, CLIP_TOK, INNER),
            shape(2, HALO, INNER),
            shape(2, HALO, INNER),
        ),
        in_specs=[VM] * (len(pieces) + 3),
        out_specs=(VM, VM, VM),
        scratch_shapes=[pltpu.VMEM((CLIP_TOK, D), BF16)],
        compiler_params=params(7),
        cost_estimate=pl.CostEstimate(
            flops=2 * CLIP_TOK * D * 3 * INNER,
            transcendentals=0,
            bytes_accessed=2 * (3 * D * INNER + CLIP_TOK * D),
        ),
        name="qkv",
    )(*pieces, gain, w, qkg)


def halo_mask(halo, which):
    parity = parity_of(which)
    seen = halo[parity]
    end = jnp.where(parity == 0, 0, lax.axis_size("clip") - 1)
    exists = jnp.where(lax.axis_index("clip") == end, 0, 1)
    lane = lax.broadcasted_iota(jnp.int32, (1, 2 * HALO), 1)
    mask = jnp.zeros((1, 2 * HALO), F32)
    for side, count in enumerate((seen, seen * exists)):
        prev = parity if side == 0 else 1 - parity
        low = side * HALO + prev * (HALO - 16 * count)
        mask = jnp.where(lane >= low, jnp.where(lane < low + 16 * count, 1.0, mask), mask)
    return mask


def attend_clip(cl, mask, mine, inner, outer, ctx, put, at=0):
    factor = math.log2(math.e) / math.sqrt(HD)
    tn = (((1,), (1,)), ((), ()))

    def step(h, carry):
        cols = pl.ds(pl.multiple_of(h * HD, HD), HD)
        q = mine[0, :, cols]
        rows = []
        for kv in range(2):
            parts = [mine[1 + kv, :, cols]]
            for ref in ctx:
                parts.append(ref[:, cl, kv, :, cols].reshape(-1, HD))
            rows.append(jnp.concatenate(parts, axis=0))
        k, v = rows
        kh = jnp.concatenate([inner[0, :, cols], outer[at, :, cols]], axis=0)
        vh = jnp.concatenate([inner[1, :, cols], outer[at + 1, :, cols]], axis=0)
        v = jnp.concatenate([v, jnp.ones_like(v)], axis=1)
        vh = jnp.concatenate([vh, jnp.ones_like(vh)], axis=1)
        s = lax.dot_general(q, k, tn, preferred_element_type=F32)
        sh = lax.dot_general(q, kh, tn, preferred_element_type=F32)
        p = jnp.exp2(s * factor).astype(BF16)
        ph = (jnp.exp2(sh * factor) * mask).astype(BF16)
        r = jnp.dot(p, v, preferred_element_type=F32)
        r = r + jnp.dot(ph, vh, preferred_element_type=F32)
        put(cols, (r[:, :HD] / r[:, HD:]).astype(BF16))
        return carry

    lax.fori_loop(0, HL, step, 0)


def attend_cost(clips, ctx):
    keys = CLIP_TOK + 2 * HALO + sum(c.shape[0] * c.shape[3] for c in ctx)
    return pl.CostEstimate(
        flops=clips * 6 * CLIP_TOK * keys * INNER,
        transcendentals=clips * HL * CLIP_TOK * keys,
        bytes_accessed=4 * keys * INNER + clips * 4 * CLIP_TOK * INNER,
    )


def attend_kernel(cl, which, halo, mine, inner, outer, c0, c1, c2, c3, out):
    def put(cols, a):
        out[0, :, cols] = a[:BLK]
        out[1, :, cols] = a[BLK:]

    ctx = (c0, c1, c2, c3)
    attend_clip(cl, halo_mask(halo, which), mine, inner, outer, ctx, put)


def attend(cl, which, halo, mine, inner, outer, ctx):
    return pl.pallas_call(
        functools.partial(attend_kernel, cl, which),
        out_shape=shape(2, BLK, INNER),
        in_specs=[SM] + [VM] * 7,
        out_specs=VM,
        compiler_params=params(7),
        cost_estimate=attend_cost(1, ctx),
        name="attend",
    )(halo, mine, inner, outer, *ctx)


def attend_pair_kernel(cl, at, *refs):
    (halo, qo, io, eo, qp, ip, ep) = refs[:7]
    ctx, (o0, o1, p0, p1) = refs[7:11], refs[11:]
    for which, args, (low, high) in (
        (0, (qo, ip, eo), (o0, o1)),
        (1, (qp, io, ep), (p0, p1)),
    ):

        def put(cols, a, low=low, high=high):
            low[:, cols] = a[:BLK]
            high[:, cols] = a[BLK:]

        attend_clip(cl, halo_mask(halo, which), *args, ctx, put, at)


def attend_pair(cl, at, halo, own, par, outer_own, outer_par, ctx):
    return pl.pallas_call(
        functools.partial(attend_pair_kernel, cl, at),
        out_shape=(shape(BLK, INNER),) * 4,
        in_specs=[SM] + [VM] * 10,
        out_specs=(VM,) * 4,
        compiler_params=params(7),
        cost_estimate=attend_cost(2, ctx),
        name="attend_pair",
    )(halo, own[0], own[2], outer_own, par[0], par[2], outer_par, *ctx)


def first_kernel(*refs):
    (o0, p0, o1, p1, o2, p2, o3, p3) = refs[:8]
    xs, refs = refs[8:-16], refs[-16:]
    (wslot, gain, w, qkg, ci) = refs[:5]
    (first, qo, eo, io, qp, ep, ip, ctx) = refs[5:13]
    (acat, xbuf, normed) = refs[13:]
    for j, (ao, ap) in enumerate(((o0, p0), (o1, p1), (p2, o2), (p3, o3))):
        for clip, piece in enumerate((ao, ap)):
            for b in range(2):
                row = (2 * clip + b) * BLK
                acat[row : row + BLK, j * INNER : (j + 1) * INNER] = piece[b ^ (j & 1)]
    rows = 2 * CLIP_TOK

    def block(k, carry):
        cols = pl.ds(quarter(place()[3], k), QUART)
        row = 0
        for x in xs:
            if row % CLIP_TOK == 0:
                left = acat[row : row + CLIP_TOK, :]
                t = jnp.dot(left, wslot[k], preferred_element_type=F32)
            end = row + x.shape[0]
            base = row - row % CLIP_TOK
            v = x[:, cols].astype(F32) + t[row - base : end - base]
            xbuf[row:end, cols] = v.astype(BF16)
            row = end
        return carry

    lax.fori_loop(0, 4, block, 0)
    first[...] = xbuf[:BLK, :]
    norm_rows([xbuf], gain.at[1:2], normed, 2)

    def put(m, c, p):
        @pl.when(m == 0)
        def _():
            qo[c] = p

        @pl.when(m == 1)
        def _():
            qp[c] = p

    project(normed, w, 1, qkg, put, rows)
    col = lax.broadcasted_iota(jnp.int32, (CLIP_TOK, CTX), 0)
    found = []
    for which, (q, e, i) in enumerate(((qo, eo, io), (qp, ep, ip))):
        put_edges(which, lambda kv, at, q=q: q[1 + kv, at, :], e, i)
        idx = jnp.where(parity_of(which) == 0, ci[0:1, :], ci[1:2, :])
        rel = ((idx // BLK) ^ place()[0]) * BLK + idx % BLK
        hot = jnp.where(col == rel, 1.0, 0.0).astype(BF16)
        tt = (((0,), (0,)), ((), ()))
        found.append(
            [
                lax.dot_general(hot, q[1 + kv], tt, preferred_element_type=F32)
                for kv in range(2)
            ]
        )
    for kv in range(2):
        both = jnp.concatenate([found[0][kv], found[1][kv]], axis=0)
        ctx[0, 0, kv] = both.astype(BF16)


def first_qkv(atts, xs, wslot, gain, w, qkg, ci):
    one = (
        shape(3, CLIP_TOK, INNER),
        shape(2, HALO, INNER),
        shape(2, HALO, INNER),
    )
    rows = 2 * CLIP_TOK
    res = pl.pallas_call(
        first_kernel,
        out_shape=(shape(BLK, D),) + one + one + (shape(1, 1, 2, 2 * CTX, INNER),),
        in_specs=[VM] * (13 + len(xs)),
        out_specs=(VM,) * 8,
        scratch_shapes=[
            pltpu.VMEM((rows, 4 * INNER), BF16),
            pltpu.VMEM((rows, D), BF16),
            pltpu.VMEM((rows, D), BF16),
        ],
        compiler_params=params(14),
        cost_estimate=pl.CostEstimate(
            flops=2 * rows * D * 7 * INNER,
            transcendentals=0,
            bytes_accessed=2 * (7 * D * INNER + 2 * rows * D),
        ),
        name="first_qkv",
    )(*atts, *xs, wslot, gain, w, qkg, ci)
    return res[0], res[1:4], res[4:7], res[7]


def final_kernel(*refs):
    skip, atts, others = refs[0], refs[1:5], refs[5:9]
    (video, first, wslot, out, acat) = refs[9:]
    for j in range(4):
        for b, piece in enumerate((atts[j], others[j])):
            acat[b * BLK : (b + 1) * BLK, j * INNER : (j + 1) * INNER] = piece[...]
    skip_first = skip[place()[1]] == 0

    def block(k, carry):
        cols = pl.ds(quarter(place()[2], k), QUART)
        t = jnp.dot(acat[...], wslot[k], preferred_element_type=F32)
        f = first[:, cols].astype(F32)
        strong = (f + t[:BLK]).astype(BF16).astype(F32)
        other = (video[:, cols].astype(F32) + t[BLK:]).astype(BF16).astype(F32)
        weak = jnp.where(skip_first, other, f)
        out[:, cols] = (strong + GUIDE * (strong - weak)).astype(BF16)
        return carry

    lax.fori_loop(0, 4, block, 0)


def final(skip, atts, others, video, first, wslot):
    return pl.pallas_call(
        final_kernel,
        out_shape=shape(BLK, D),
        in_specs=[SM] + [VM] * 11,
        out_specs=VM,
        scratch_shapes=[pltpu.VMEM((2 * BLK, 4 * INNER), BF16)],
        compiler_params=params(7),
        cost_estimate=pl.CostEstimate(
            flops=4 * BLK * D * 4 * INNER,
            transcendentals=0,
            bytes_accessed=2 * (4 * D * INNER + 3 * BLK * D),
        ),
        name="final",
    )(skip, *atts, *others, video, first, wslot)


def after(value, *done):
    return lax.optimization_barrier((value,) + done)[0]


def columns_kernel(wo, *refs):
    outs, sems = refs[:2], refs[2]
    copies = []
    for l in range(2):
        cols = pl.ds(pl.multiple_of(place()[3 - l] * QUART, QUART), QUART)
        copies.append(
            pltpu.make_async_copy(wo.at[l, :, cols], outs[l], sems.at[l])
        )
    for copy in copies:
        copy.start()
    for copy in copies:
        copy.wait()


def columns(weight):
    return pl.pallas_call(
        columns_kernel,
        out_shape=(shape(INNER, QUART),) * 2,
        in_specs=[pl.BlockSpec(memory_space=pltpu.HBM)],
        out_specs=(VM, VM),
        scratch_shapes=[pltpu.SemaphoreType.DMA((2,))],
        compiler_params=params(3),
        name="columns",
    )(weight)


def edges(own, par):
    return send(par[1], edge_par), send(own[1], edge_own)


def body(video, norm_gain, w_qkv, qk_gain, w_out, skip_layer, halo_frames, context_index):
    x0 = video
    piece0, piece1 = columns(pltpu.with_memory_space_constraint(w_out, pltpu.HBM))
    here0 = send(piece0, to_far_z)
    c0, xa, xb = context_rows(context_index, after(x0, piece0))
    c = [c0, send(c0, to_sib), send(c0, to_z), send(c0, to_diag)]
    x2a = send(xa, to_z)
    x1 = send(after(x0, c0), to_sib)
    w = stage(pltpu.with_memory_space_constraint(jnp.transpose(w_qkv, (0, 2, 1, 3)), pltpu.HBM))
    kv = context_kv(c, norm_gain, w, qk_gain)
    kz = send(kv, to_far)
    x2b = send(after(xb, kv), to_z)
    wz0 = [here0] + [send(after(here0, kv), to_y(d)) for d in (1, 3)]
    own0 = qkv(0, 0, (after(x0, kv), x1), norm_gain, w, qk_gain)
    kx = pack(kv, after(kz, own0[0]))
    kxs = [send(kx, to_x(d)) for d in (1, 3, 2)]
    x3a = send(after(x2a, kx), to_sib)
    here1 = send(after(piece1, kx), to_far_z)
    own1 = qkv(1, 0, (after(x0, kx), x1), norm_gain, w, qk_gain)
    ky = pack(kx, *[after(k, own1[0]) for k in kxs])
    kys = [send(ky, to_y(d)) for d in (1, 3, 2)]
    x3b = send(after(x2b, own1[0]), to_sib)
    halves = (after(x2a, ky), x2b, x3a, x3b)
    par0 = qkv(0, 1, halves, norm_gain, w, qk_gain)
    eo, ep = edges(own0, par0)
    wsib = send(after(w_out, par0[0]), to_sib)
    wz0.append(send(after(here0, par0[0]), to_y(2)))
    wz1 = [here1] + [send(after(here1, eo, ep), to_x(d)) for d in (1, 3, 2)]
    ctx = [ky] + kys
    ao = attend(0, 0, halo_frames, own0[0], par0[2], eo, ctx)
    oz = send(ao, to_z)
    os = send(ao, to_sib)
    ap = attend(0, 1, halo_frames, after(par0[0], ao), own0[2], ep, ctx)
    pz = send(ap, to_z)
    ps = send(ap, to_sib)
    halves = (after(x2a, ap), x2b, x3a, x3b)
    par1 = qkv(1, 1, halves, norm_gain, w, qk_gain)
    wzs0 = [send(after(p, ap), to_sib) for p in wz0]
    ozs = send(after(oz, par1[0]), to_sib)
    wslot0 = assemble(0, after(w_out, par1[0]), wsib, wz0, wzs0)
    pzs = send(pz, to_sib)

    first, fo, fp, fkv = first_qkv(
        (ao, ap, os, ps, oz, pz, ozs, pzs),
        (x0, x1, x2a, x2b, x3a, x3b),
        wslot0,
        norm_gain,
        w,
        qk_gain,
        context_index,
    )
    fz = send(fkv, to_far)
    both_own = pack(own1[1], fo[1])
    both_par = pack(par1[1], fp[1])
    fx = pack(fkv, fz)
    fxs = [send(fx, to_x(d)) for d in (1, 3, 2)]
    so, sp = edges((None, after(both_own, fx)), (None, after(both_par, fx)))
    fy = pack(fx, *fxs)
    fys = [send(fy, to_y(d)) for d in (1, 3, 2)]
    mine = (after(own1[0], fy),) + own1[1:]
    b = attend_pair(1, 0, halo_frames, mine, par1, so, sp, ctx)
    others = [b[0], send(b[1], to_sib), send(b[2], to_z), send(b[3], to_diag)]
    mine = (after(fo[0], b[0]),) + fo[1:]
    g = attend_pair(0, 2, halo_frames, mine, fp, so, sp, [fy] + fys)
    atts = [g[0], send(g[1], to_sib), send(g[2], to_z), send(g[3], to_diag)]
    wzs1 = [send(after(p, b[0]), to_sib) for p in wz1]
    wslot1 = assemble(1, after(w_out, g[0]), wsib, wz1, wzs1)
    return final(skip_layer, atts, others, x0, first, wslot1)


def solution(mesh):
    in_specs = (
        P(("clip", "head"), None),
        P(),
        P(None, None, None, "head"),
        P(),
        P(None, "head", None),
        P("clip"),
        P("clip"),
        P("clip", None),
    )
    out_specs = P(("clip", "head"), None)

    return jax.shard_map(
        body, mesh=mesh, in_specs=in_specs, out_specs=out_specs, check_vma=False
    )
```

```python
import functools
import math

import jax
import jax.numpy as jnp
from jax import lax
from jax.experimental import pallas as pl
from jax.experimental.pallas import tpu as pltpu
from jax.sharding import PartitionSpec as P


D = 3072
HD = 128
HL = 3
INNER = HL * HD
BLK = 128
CLIP_TOK = 256
CTX = 8
HALO = 32
QUART = D // 4
GUIDE = 1.5
EPS = 1e-06
AXES = ("clip", "head")
F32, BF16 = jnp.float32, jnp.bfloat16
ANY = pl.BlockSpec(memory_space=pl.ANY)
VM = pl.BlockSpec(memory_space=pltpu.VMEM)
SM = pl.BlockSpec(memory_space=pltpu.SMEM)


def moved(clips, heads, rule):
    pairs = []
    for c in range(clips):
        for h in range(heads):
            to = rule(c, h)
            if to is not None:
                pairs.append((c * heads + h, to[0] * heads + to[1]))
    return pairs


def send(value, rule):
    pairs = moved(lax.axis_size("clip"), lax.axis_size("head"), rule)
    return lax.ppermute(value, AXES, pairs)


def to_sib(c, h):
    return c, h ^ 1


def to_z(c, h):
    return c, h ^ 2


def to_diag(c, h):
    return c, h ^ 3


def to_far(c, h):
    return c ^ 16, h


def to_far_z(c, h):
    return c ^ 16, h ^ 2


def to_x(step):
    return lambda c, h: ((c & ~3) | ((c + step) & 3), h)


def to_y(step):
    return lambda c, h: ((c & ~12) | ((c + 4 * step) & 12), h)


def edge_own(c, h):
    to = c - 1 if h < 2 else c + 1
    return (to, h) if 0 <= to < 32 else None


def edge_par(c, h):
    to = c + 1 if h < 2 else c - 1
    return (to, h) if 0 <= to < 32 else None


def shape(*dims):
    return jax.ShapeDtypeStruct(dims, BF16)


def params(mib):
    return pltpu.CompilerParams(vmem_limit_bytes=mib * 1024 * 1024)


def pack_kernel(*refs):
    out = refs[-1]
    step = out.shape[0] // (len(refs) - 1)
    for i, ref in enumerate(refs[:-1]):
        out[i * step : (i + 1) * step] = ref[...]


def pack(*parts):
    lead, rest = parts[0].shape[0], parts[0].shape[1:]
    return pl.pallas_call(
        pack_kernel,
        out_shape=shape(len(parts) * lead, *rest),
        in_specs=[VM] * len(parts),
        out_specs=VM,
        compiler_params=params(4),
        name="pack",
    )(*parts)


def quarter(turn, k):
    off = jnp.where(k == 0, 0, jnp.where(k == 1, 3, k - 1))
    return pl.multiple_of(((turn + off) & 3) * QUART, QUART)


def stage_kernel(w, out, sems):
    copies = [
        pltpu.make_async_copy(
            w.at[l, c], out.at[l, :, pl.ds(c * INNER, INNER)], sems.at[3 * l + c]
        )
        for l in range(2)
        for c in range(3)
    ]
    for copy in copies:
        copy.start()
    for copy in copies:
        copy.wait()


def stage(w):
    return pl.pallas_call(
        stage_kernel,
        out_shape=pltpu.VMEM((2, D, 3 * INNER), BF16),
        in_specs=[pl.BlockSpec(memory_space=pltpu.HBM)],
        out_specs=VM,
        scratch_shapes=[pltpu.SemaphoreType.DMA((6,))],
        compiler_params=params(2),
        name="stage",
    )(w)


def assemble_kernel(layer, wo, wsib, *refs):
    wz, wzs, out, sems = refs[:4], refs[4:8], refs[8], refs[9]
    copies = []
    for k in range(4):
        cols = pl.ds(quarter(place()[3 - layer], k), QUART)
        for j, src in enumerate(
            (wo.at[layer, :, cols], wsib.at[layer, :, cols], wz[k], wzs[k])
        ):
            dst = out.at[k, pl.ds(j * INNER, INNER)]
            copies.append(pltpu.make_async_copy(src, dst, sems.at[4 * k + j]))
    for copy in copies:
        copy.start()
    for copy in copies:
        copy.wait()


def assemble(layer, wo, wsib, wz, wzs):
    hbm = pl.BlockSpec(memory_space=pltpu.HBM)
    return pl.pallas_call(
        functools.partial(assemble_kernel, layer),
        out_shape=pltpu.VMEM((4, 4 * INNER, QUART), BF16),
        in_specs=[hbm] * 10,
        out_specs=VM,
        scratch_shapes=[pltpu.SemaphoreType.DMA((16,))],
        compiler_params=params(2),
        name="assemble",
    )(wo, wsib, *wz, *wzs)


def norm_rows(pieces, gain, dst, unroll=1):
    rows = pieces[0].shape[0]

    def step(i, carry):
        at = pl.ds(pl.multiple_of(i * 16, 16), 16)
        for k, src in enumerate(pieces):
            to = pl.ds(pl.multiple_of(k * rows + i * 16, 16), 16)
            v = src[at, :].astype(F32)
            ms = jnp.mean(v * v, axis=-1, keepdims=True)
            dst[to, :] = (v * lax.rsqrt(ms + EPS) * gain[...]).astype(BF16)
        return carry

    lax.fori_loop(0, rows // 16, step, 0, unroll=unroll)


def head_norm(p, gain):
    parts = []
    for h in range(HL):
        ph = p[:, h * HD : (h + 1) * HD]
        ms = jnp.mean(ph * ph, axis=-1, keepdims=True)
        parts.append(ph * lax.rsqrt(ms + EPS) * gain)
    return jnp.concatenate(parts, axis=1)


def project(normed, w, l, qkg, put, rows):
    def step(m, carry):
        row = pl.multiple_of(m * CLIP_TOK, CLIP_TOK)
        p = jnp.dot(
            normed[pl.ds(row, CLIP_TOK), :], w[l], preferred_element_type=F32
        )
        for c in range(3):
            pc = p[:, c * INNER : (c + 1) * INNER]
            if c < 2:
                pc = head_norm(pc, qkg[l, c : c + 1, :])
            put(m, c, pc.astype(BF16))
        return carry

    lax.fori_loop(0, rows // CLIP_TOK, step, 0)


def place():
    clip, head = lax.axis_index("clip"), lax.axis_index("head")
    return head & 1, head >> 1, clip & 3, (clip >> 2) & 3


def parity_of(which):
    zlo = place()[1]
    return zlo if which == 0 else 1 - zlo


def put_edges(which, rows, outer, inner):
    core, parity = place()[0], parity_of(which)
    for edge, last in ((outer, parity), (inner, 1 - parity)):
        start = pl.multiple_of((last ^ core) * BLK + last * (BLK - HALO), HALO)
        for kv in range(2):
            edge[kv] = rows(kv, pl.ds(start, HALO))


def rows_kernel(ci, x, out, low, high):
    low[...] = x[: BLK // 2, :]
    high[...] = x[BLK // 2 :, :]
    core, zlo = place()[:2]
    row = lax.broadcasted_iota(jnp.int32, (8, BLK), 0)
    col = lax.broadcasted_iota(jnp.int32, (8, BLK), 1)
    at = jnp.full((8, BLK), -1, jnp.int32)
    for r in range(4):
        at = jnp.where(row == r, ci[zlo, 4 * core + r] - core * BLK, at)
    hot = jnp.where(col == at, 1.0, 0.0).astype(BF16)
    got = jnp.dot(hot, x[...], preferred_element_type=F32)
    out[...] = got[:4].astype(BF16)


def context_rows(ci, x):
    return pl.pallas_call(
        rows_kernel,
        out_shape=(shape(4, D), shape(BLK // 2, D), shape(BLK // 2, D)),
        in_specs=[SM, VM],
        out_specs=(VM, VM, VM),
        compiler_params=params(4),
        name="context_rows",
    )(ci, x)


def context_kernel(c0, c1, c2, c3, gain, w, qkg, out, xs, normed):
    for j, c in enumerate((c0, c1, c2, c3)):
        xs[4 * j : 4 * j + 4, :] = c[...].astype(F32)
    v = xs[...]
    v = v * lax.rsqrt(jnp.mean(v * v, axis=-1, keepdims=True) + EPS)
    xs[...] = v

    def step(l, carry):
        normed[...] = (xs[...] * gain[pl.ds(l, 1), :]).astype(BF16)
        p = jnp.dot(normed[...], w[l, :, INNER:], preferred_element_type=F32)
        out[0, l, 0] = head_norm(p[:, :INNER], qkg[l, 1:2, :]).astype(BF16)
        out[0, l, 1] = p[:, INNER:].astype(BF16)
        return carry

    lax.fori_loop(0, 2, step, 0)


def context_kv(c, gain, w, qkg):
    return pl.pallas_call(
        context_kernel,
        out_shape=shape(1, 2, 2, 2 * CTX, INNER),
        in_specs=[VM] * 7,
        out_specs=VM,
        scratch_shapes=[
            pltpu.VMEM((2 * CTX, D), F32),
            pltpu.VMEM((2 * CTX, D), BF16),
        ],
        compiler_params=params(4),
        cost_estimate=pl.CostEstimate(
            flops=2 * 256 * D * 4 * INNER, transcendentals=0, bytes_accessed=8 * D * INNER
        ),
        name="context_kv",
    )(*c, gain, w, qkg)


def qkv_kernel(l, which, *refs):
    pieces, (gain, w, qkg, out, outer, inner, normed) = refs[:-7], refs[-7:]
    half = BLK // 2
    views = [p.at[pl.ds(r, half)] for p in pieces for r in range(0, p.shape[0], half)]
    norm_rows(views, gain.at[l : l + 1], normed)

    def put(m, c, p):
        out[c] = p

    project(normed, w, l, qkg, put, CLIP_TOK)
    put_edges(which, lambda kv, at: out[1 + kv, at, :], outer, inner)


def qkv(l, which, pieces, gain, w, qkg):
    return pl.pallas_call(
        functools.partial(qkv_kernel, l, which),
        out_shape=(
            shape(3, CLIP_TOK, INNER),
            shape(2, HALO, INNER),
            shape(2, HALO, INNER),
        ),
        in_specs=[VM] * (len(pieces) + 3),
        out_specs=(VM, VM, VM),
        scratch_shapes=[pltpu.VMEM((CLIP_TOK, D), BF16)],
        compiler_params=params(7),
        cost_estimate=pl.CostEstimate(
            flops=2 * CLIP_TOK * D * 3 * INNER,
            transcendentals=0,
            bytes_accessed=2 * (3 * D * INNER + CLIP_TOK * D),
        ),
        name="qkv",
    )(*pieces, gain, w, qkg)


def halo_mask(halo, which):
    parity = parity_of(which)
    seen = halo[parity]
    end = jnp.where(parity == 0, 0, lax.axis_size("clip") - 1)
    exists = jnp.where(lax.axis_index("clip") == end, 0, 1)
    lane = lax.broadcasted_iota(jnp.int32, (1, 2 * HALO), 1)
    mask = jnp.zeros((1, 2 * HALO), F32)
    for side, count in enumerate((seen, seen * exists)):
        prev = parity if side == 0 else 1 - parity
        low = side * HALO + prev * (HALO - 16 * count)
        mask = jnp.where(lane >= low, jnp.where(lane < low + 16 * count, 1.0, mask), mask)
    return mask


def attend_clip(cl, mask, mine, inner, outer, ctx, put, at=0):
    factor = math.log2(math.e) / math.sqrt(HD)
    tn = (((1,), (1,)), ((), ()))

    def step(h, carry):
        cols = pl.ds(pl.multiple_of(h * HD, HD), HD)
        q = mine[0, :, cols]
        rows = []
        for kv in range(2):
            parts = [mine[1 + kv, :, cols]]
            for ref in ctx:
                parts.append(ref[:, cl, kv, :, cols].reshape(-1, HD))
            rows.append(jnp.concatenate(parts, axis=0))
        k, v = rows
        kh = jnp.concatenate([inner[0, :, cols], outer[at, :, cols]], axis=0)
        vh = jnp.concatenate([inner[1, :, cols], outer[at + 1, :, cols]], axis=0)
        v = jnp.concatenate([v, jnp.ones_like(v)], axis=1)
        vh = jnp.concatenate([vh, jnp.ones_like(vh)], axis=1)
        s = lax.dot_general(q, k, tn, preferred_element_type=F32)
        sh = lax.dot_general(q, kh, tn, preferred_element_type=F32)
        p = jnp.exp2(s * factor).astype(BF16)
        ph = (jnp.exp2(sh * factor) * mask).astype(BF16)
        r = jnp.dot(p, v, preferred_element_type=F32)
        r = r + jnp.dot(ph, vh, preferred_element_type=F32)
        put(cols, (r[:, :HD] / r[:, HD:]).astype(BF16))
        return carry

    lax.fori_loop(0, HL, step, 0)


def attend_cost(clips, ctx):
    keys = CLIP_TOK + 2 * HALO + sum(c.shape[0] * c.shape[3] for c in ctx)
    return pl.CostEstimate(
        flops=clips * 6 * CLIP_TOK * keys * INNER,
        transcendentals=clips * HL * CLIP_TOK * keys,
        bytes_accessed=4 * keys * INNER + clips * 4 * CLIP_TOK * INNER,
    )


def attend_kernel(cl, which, halo, mine, inner, outer, c0, c1, c2, c3, out):
    def put(cols, a):
        out[0, :, cols] = a[:BLK]
        out[1, :, cols] = a[BLK:]

    ctx = (c0, c1, c2, c3)
    attend_clip(cl, halo_mask(halo, which), mine, inner, outer, ctx, put)


def attend(cl, which, halo, mine, inner, outer, ctx):
    return pl.pallas_call(
        functools.partial(attend_kernel, cl, which),
        out_shape=shape(2, BLK, INNER),
        in_specs=[SM] + [VM] * 7,
        out_specs=VM,
        compiler_params=params(7),
        cost_estimate=attend_cost(1, ctx),
        name="attend",
    )(halo, mine, inner, outer, *ctx)


def attend_pair_kernel(cl, at, *refs):
    (halo, qo, io, eo, qp, ip, ep) = refs[:7]
    ctx, (o0, o1, p0, p1) = refs[7:11], refs[11:]
    for which, args, (low, high) in (
        (0, (qo, ip, eo), (o0, o1)),
        (1, (qp, io, ep), (p0, p1)),
    ):

        def put(cols, a, low=low, high=high):
            low[:, cols] = a[:BLK]
            high[:, cols] = a[BLK:]

        attend_clip(cl, halo_mask(halo, which), *args, ctx, put, at)


def attend_pair(cl, at, halo, own, par, outer_own, outer_par, ctx):
    return pl.pallas_call(
        functools.partial(attend_pair_kernel, cl, at),
        out_shape=(shape(BLK, INNER),) * 4,
        in_specs=[SM] + [VM] * 10,
        out_specs=(VM,) * 4,
        compiler_params=params(7),
        cost_estimate=attend_cost(2, ctx),
        name="attend_pair",
    )(halo, own[0], own[2], outer_own, par[0], par[2], outer_par, *ctx)


def first_kernel(*refs):
    (o0, p0, o1, p1, o2, p2, o3, p3) = refs[:8]
    xs, refs = refs[8:-16], refs[-16:]
    (wslot, gain, w, qkg, ci) = refs[:5]
    (first, qo, eo, io, qp, ep, ip, ctx) = refs[5:13]
    (acat, xbuf, normed) = refs[13:]
    for j, (ao, ap) in enumerate(((o0, p0), (o1, p1), (p2, o2), (p3, o3))):
        for clip, piece in enumerate((ao, ap)):
            for b in range(2):
                row = (2 * clip + b) * BLK
                acat[row : row + BLK, j * INNER : (j + 1) * INNER] = piece[b ^ (j & 1)]
    rows = 2 * CLIP_TOK

    def block(k, carry):
        cols = pl.ds(quarter(place()[3], k), QUART)
        row = 0
        for x in xs:
            if row % CLIP_TOK == 0:
                left = acat[row : row + CLIP_TOK, :]
                t = jnp.dot(left, wslot[k], preferred_element_type=F32)
            end = row + x.shape[0]
            base = row - row % CLIP_TOK
            v = x[:, cols].astype(F32) + t[row - base : end - base]
            xbuf[row:end, cols] = v.astype(BF16)
            row = end
        return carry

    lax.fori_loop(0, 4, block, 0)
    first[...] = xbuf[:BLK, :]
    norm_rows([xbuf], gain.at[1:2], normed, 2)

    def put(m, c, p):
        @pl.when(m == 0)
        def _():
            qo[c] = p

        @pl.when(m == 1)
        def _():
            qp[c] = p

    project(normed, w, 1, qkg, put, rows)
    col = lax.broadcasted_iota(jnp.int32, (CLIP_TOK, CTX), 0)
    found = []
    for which, (q, e, i) in enumerate(((qo, eo, io), (qp, ep, ip))):
        put_edges(which, lambda kv, at, q=q: q[1 + kv, at, :], e, i)
        idx = jnp.where(parity_of(which) == 0, ci[0:1, :], ci[1:2, :])
        rel = ((idx // BLK) ^ place()[0]) * BLK + idx % BLK
        hot = jnp.where(col == rel, 1.0, 0.0).astype(BF16)
        tt = (((0,), (0,)), ((), ()))
        found.append(
            [
                lax.dot_general(hot, q[1 + kv], tt, preferred_element_type=F32)
                for kv in range(2)
            ]
        )
    for kv in range(2):
        both = jnp.concatenate([found[0][kv], found[1][kv]], axis=0)
        ctx[0, 0, kv] = both.astype(BF16)


def first_qkv(atts, xs, wslot, gain, w, qkg, ci):
    one = (
        shape(3, CLIP_TOK, INNER),
        shape(2, HALO, INNER),
        shape(2, HALO, INNER),
    )
    rows = 2 * CLIP_TOK
    res = pl.pallas_call(
        first_kernel,
        out_shape=(shape(BLK, D),) + one + one + (shape(1, 1, 2, 2 * CTX, INNER),),
        in_specs=[VM] * (13 + len(xs)),
        out_specs=(VM,) * 8,
        scratch_shapes=[
            pltpu.VMEM((rows, 4 * INNER), BF16),
            pltpu.VMEM((rows, D), BF16),
            pltpu.VMEM((rows, D), BF16),
        ],
        compiler_params=params(14),
        cost_estimate=pl.CostEstimate(
            flops=2 * rows * D * 7 * INNER,
            transcendentals=0,
            bytes_accessed=2 * (7 * D * INNER + 2 * rows * D),
        ),
        name="first_qkv",
    )(*atts, *xs, wslot, gain, w, qkg, ci)
    return res[0], res[1:4], res[4:7], res[7]


def final_kernel(*refs):
    skip, atts, others = refs[0], refs[1:5], refs[5:9]
    (xa, xb, first, wslot, out, acat) = refs[9:]
    for j in range(4):
        for b, piece in enumerate((atts[j], others[j])):
            acat[b * BLK : (b + 1) * BLK, j * INNER : (j + 1) * INNER] = piece[...]
    skip_first = skip[place()[1]] == 0

    def block(k, carry):
        cols = pl.ds(quarter(place()[2], k), QUART)
        t = jnp.dot(acat[...], wslot[k], preferred_element_type=F32)
        f = first[:, cols].astype(F32)
        strong = (f + t[:BLK]).astype(BF16).astype(F32)
        video = jnp.concatenate([xa[:, cols], xb[:, cols]], axis=0).astype(F32)
        other = (video + t[BLK:]).astype(BF16).astype(F32)
        weak = jnp.where(skip_first, other, f)
        out[:, cols] = (strong + GUIDE * (strong - weak)).astype(BF16)
        return carry

    lax.fori_loop(0, 4, block, 0)


def final(skip, atts, others, xa, xb, first, wslot):
    return pl.pallas_call(
        final_kernel,
        out_shape=shape(BLK, D),
        in_specs=[SM] + [VM] * 12,
        out_specs=VM,
        scratch_shapes=[pltpu.VMEM((2 * BLK, 4 * INNER), BF16)],
        compiler_params=params(7),
        cost_estimate=pl.CostEstimate(
            flops=4 * BLK * D * 4 * INNER,
            transcendentals=0,
            bytes_accessed=2 * (4 * D * INNER + 3 * BLK * D),
        ),
        name="final",
    )(skip, *atts, *others, xa, xb, first, wslot)


def after(value, *done):
    return lax.optimization_barrier((value,) + done)[0]


def columns_kernel(wo, *refs):
    outs, sems = refs[:2], refs[2]
    copies = []
    for l in range(2):
        cols = pl.ds(pl.multiple_of(place()[3 - l] * QUART, QUART), QUART)
        copies.append(
            pltpu.make_async_copy(wo.at[l, :, cols], outs[l], sems.at[l])
        )
    for copy in copies:
        copy.start()
    for copy in copies:
        copy.wait()


def columns(weight):
    return pl.pallas_call(
        columns_kernel,
        out_shape=(shape(INNER, QUART),) * 2,
        in_specs=[pl.BlockSpec(memory_space=pltpu.HBM)],
        out_specs=(VM, VM),
        scratch_shapes=[pltpu.SemaphoreType.DMA((2,))],
        compiler_params=params(3),
        name="columns",
    )(weight)


def edges(own, par):
    return send(par[1], edge_par), send(own[1], edge_own)


def body(video, norm_gain, w_qkv, qk_gain, w_out, skip_layer, halo_frames, context_index):
    x0 = video
    piece0, piece1 = columns(pltpu.with_memory_space_constraint(w_out, pltpu.HBM))
    here0 = send(piece0, to_far_z)
    c0, xa, xb = context_rows(context_index, after(x0, piece0))
    c = [c0, send(c0, to_sib), send(c0, to_z), send(c0, to_diag)]
    x2a = send(xa, to_z)
    x1 = send(after(x0, c0), to_sib)
    w = stage(pltpu.with_memory_space_constraint(jnp.transpose(w_qkv, (0, 2, 1, 3)), pltpu.HBM))
    kv = context_kv(c, norm_gain, w, qk_gain)
    kz = send(kv, to_far)
    x2b = send(after(xb, kv), to_z)
    wz0 = [here0] + [send(after(here0, kv), to_y(d)) for d in (1, 3)]
    own0 = qkv(0, 0, (after(xa, kv), xb, x1), norm_gain, w, qk_gain)
    kx = pack(kv, after(kz, own0[0]))
    kxs = [send(kx, to_x(d)) for d in (1, 3, 2)]
    x3a = send(after(x2a, kx), to_sib)
    own1 = qkv(1, 0, (after(xa, kx), xb, x1), norm_gain, w, qk_gain)
    ky = pack(kx, *[after(k, own1[0]) for k in kxs])
    kys = [send(ky, to_y(d)) for d in (1, 3, 2)]
    here1 = send(after(piece1, ky), to_far_z)
    x3b = send(after(x2b, own1[0]), to_sib)
    halves = (after(x2a, ky), x2b, x3a, x3b)
    par0 = qkv(0, 1, halves, norm_gain, w, qk_gain)
    eo, ep = edges(own0, par0)
    wsib = send(after(w_out, par0[0]), to_sib)
    ctx = [ky] + kys
    ao = attend(0, 0, halo_frames, own0[0], par0[2], eo, ctx)
    wz0.append(send(after(here0, ao), to_y(2)))
    oz = send(ao, to_z)
    os = send(ao, to_sib)
    ap = attend(0, 1, halo_frames, after(par0[0], ao), own0[2], ep, ctx)
    pz = send(ap, to_z)
    ps = send(ap, to_sib)
    halves = (after(x2a, ap), x2b, x3a, x3b)
    par1 = qkv(1, 1, halves, norm_gain, w, qk_gain)
    wzs0 = [send(after(p, ap), to_sib) for p in wz0[:3]]
    wzs0.append(send(after(wz0[3], par1[0]), to_sib))
    wz1 = [here1] + [send(after(here1, par1[0]), to_x(d)) for d in (1, 3, 2)]
    ozs = send(after(oz, par1[0]), to_sib)
    wslot0 = assemble(0, after(w_out, par1[0]), wsib, wz0, wzs0)
    pzs = send(pz, to_sib)

    first, fo, fp, fkv = first_qkv(
        (ao, ap, os, ps, oz, pz, ozs, pzs),
        (xa, xb, x1, x2a, x2b, x3a, x3b),
        wslot0,
        norm_gain,
        w,
        qk_gain,
        context_index,
    )
    fz = send(fkv, to_far)
    both_own = pack(own1[1], fo[1])
    both_par = pack(par1[1], fp[1])
    fx = pack(fkv, fz)
    fxs = [send(fx, to_x(d)) for d in (1, 3, 2)]
    so, sp = edges((None, after(both_own, fx)), (None, after(both_par, fx)))
    fy = pack(fx, *fxs)
    fys = [send(fy, to_y(d)) for d in (1, 3, 2)]
    mine = (after(own1[0], fy),) + own1[1:]
    b = attend_pair(1, 0, halo_frames, mine, par1, so, sp, ctx)
    others = [b[0], send(b[1], to_sib), send(b[2], to_z), send(b[3], to_diag)]
    mine = (after(fo[0], b[0]),) + fo[1:]
    g = attend_pair(0, 2, halo_frames, mine, fp, so, sp, [fy] + fys)
    atts = [g[0], send(g[1], to_sib), send(g[2], to_z), send(g[3], to_diag)]
    wzs1 = [send(after(p, b[0]), to_sib) for p in wz1]
    wslot1 = assemble(1, after(w_out, g[0]), wsib, wz1, wzs1)
    return final(skip_layer, atts, others, xa, xb, first, wslot1)


def solution(mesh):
    in_specs = (
        P(("clip", "head"), None),
        P(),
        P(None, None, None, "head"),
        P(),
        P(None, "head", None),
        P("clip"),
        P("clip"),
        P("clip", None),
    )
    out_specs = P(("clip", "head"), None)

    return jax.shard_map(
        body, mesh=mesh, in_specs=in_specs, out_specs=out_specs, check_vma=False
    )
```

```python
import functools
import math

import jax
import jax.numpy as jnp
from jax import lax
from jax.experimental import pallas as pl
from jax.experimental.pallas import tpu as pltpu
from jax.sharding import PartitionSpec as P


D = 3072
HD = 128
HL = 3
INNER = HL * HD
BLK = 128
CLIP_TOK = 256
CTX = 8
HALO = 32
QUART = D // 4
GUIDE = 1.5
EPS = 1e-06
AXES = ("clip", "head")
F32, BF16 = jnp.float32, jnp.bfloat16
ANY = pl.BlockSpec(memory_space=pl.ANY)
VM = pl.BlockSpec(memory_space=pltpu.VMEM)
SM = pl.BlockSpec(memory_space=pltpu.SMEM)


def moved(clips, heads, rule):
    pairs = []
    for c in range(clips):
        for h in range(heads):
            to = rule(c, h)
            if to is not None:
                pairs.append((c * heads + h, to[0] * heads + to[1]))
    return pairs


def send(value, rule):
    pairs = moved(lax.axis_size("clip"), lax.axis_size("head"), rule)
    return lax.ppermute(value, AXES, pairs)


def to_sib(c, h):
    return c, h ^ 1


def to_z(c, h):
    return c, h ^ 2


def to_diag(c, h):
    return c, h ^ 3


def to_far(c, h):
    return c ^ 16, h


def to_far_z(c, h):
    return c ^ 16, h ^ 2


def to_x(step):
    return lambda c, h: ((c & ~3) | ((c + step) & 3), h)


def to_y(step):
    return lambda c, h: ((c & ~12) | ((c + 4 * step) & 12), h)


def edge_own(c, h):
    to = c - 1 if h < 2 else c + 1
    return (to, h) if 0 <= to < 32 else None


def edge_par(c, h):
    to = c + 1 if h < 2 else c - 1
    return (to, h) if 0 <= to < 32 else None


def shape(*dims):
    return jax.ShapeDtypeStruct(dims, BF16)


def params(mib):
    return pltpu.CompilerParams(vmem_limit_bytes=mib * 1024 * 1024)


def pack_kernel(*refs):
    out = refs[-1]
    step = out.shape[0] // (len(refs) - 1)
    for i, ref in enumerate(refs[:-1]):
        out[i * step : (i + 1) * step] = ref[...]


def pack(*parts):
    lead, rest = parts[0].shape[0], parts[0].shape[1:]
    return pl.pallas_call(
        pack_kernel,
        out_shape=shape(len(parts) * lead, *rest),
        in_specs=[VM] * len(parts),
        out_specs=VM,
        compiler_params=params(4),
        name="pack",
    )(*parts)


def quarter(turn, k):
    off = jnp.where(k == 0, 0, jnp.where(k == 1, 3, k - 1))
    return pl.multiple_of(((turn + off) & 3) * QUART, QUART)


def stage_kernel(w, out, sems):
    copies = [
        pltpu.make_async_copy(
            w.at[l, c], out.at[l, :, pl.ds(c * INNER, INNER)], sems.at[3 * l + c]
        )
        for l in range(2)
        for c in range(3)
    ]
    for copy in copies:
        copy.start()
    for copy in copies:
        copy.wait()


def stage(w):
    return pl.pallas_call(
        stage_kernel,
        out_shape=pltpu.VMEM((2, D, 3 * INNER), BF16),
        in_specs=[pl.BlockSpec(memory_space=pltpu.HBM)],
        out_specs=VM,
        scratch_shapes=[pltpu.SemaphoreType.DMA((6,))],
        compiler_params=params(2),
        name="stage",
    )(w)


def assemble_kernel(layer, wo, wsib, *refs):
    wz, wzs, out, sems = refs[:4], refs[4:8], refs[8], refs[9]
    copies = []
    for k in range(4):
        cols = pl.ds(quarter(place()[3 - layer], k), QUART)
        for j, src in enumerate(
            (wo.at[layer, :, cols], wsib.at[layer, :, cols], wz[k], wzs[k])
        ):
            dst = out.at[k, pl.ds(j * INNER, INNER)]
            copies.append(pltpu.make_async_copy(src, dst, sems.at[4 * k + j]))
    for copy in copies:
        copy.start()
    for copy in copies:
        copy.wait()


def assemble(layer, wo, wsib, wz, wzs):
    hbm = pl.BlockSpec(memory_space=pltpu.HBM)
    return pl.pallas_call(
        functools.partial(assemble_kernel, layer),
        out_shape=pltpu.VMEM((4, 4 * INNER, QUART), BF16),
        in_specs=[hbm] * 10,
        out_specs=VM,
        scratch_shapes=[pltpu.SemaphoreType.DMA((16,))],
        compiler_params=params(2),
        name="assemble",
    )(wo, wsib, *wz, *wzs)


def norm_rows(pieces, gain, dst, unroll=1):
    rows = pieces[0].shape[0]

    def step(i, carry):
        at = pl.ds(pl.multiple_of(i * 16, 16), 16)
        for k, src in enumerate(pieces):
            to = pl.ds(pl.multiple_of(k * rows + i * 16, 16), 16)
            v = src[at, :].astype(F32)
            ms = jnp.mean(v * v, axis=-1, keepdims=True)
            dst[to, :] = (v * lax.rsqrt(ms + EPS) * gain[...]).astype(BF16)
        return carry

    lax.fori_loop(0, rows // 16, step, 0, unroll=unroll)


def head_norm(p, gain):
    parts = []
    for h in range(HL):
        ph = p[:, h * HD : (h + 1) * HD]
        ms = jnp.mean(ph * ph, axis=-1, keepdims=True)
        parts.append(ph * lax.rsqrt(ms + EPS) * gain)
    return jnp.concatenate(parts, axis=1)


def project(normed, w, l, qkg, put, rows):
    def step(m, carry):
        row = pl.multiple_of(m * CLIP_TOK, CLIP_TOK)
        p = jnp.dot(
            normed[pl.ds(row, CLIP_TOK), :], w[l], preferred_element_type=F32
        )
        for c in range(3):
            pc = p[:, c * INNER : (c + 1) * INNER]
            if c < 2:
                pc = head_norm(pc, qkg[l, c : c + 1, :])
            put(m, c, pc.astype(BF16))
        return carry

    lax.fori_loop(0, rows // CLIP_TOK, step, 0)


def place():
    clip, head = lax.axis_index("clip"), lax.axis_index("head")
    return head & 1, head >> 1, clip & 3, (clip >> 2) & 3


def parity_of(which):
    zlo = place()[1]
    return zlo if which == 0 else 1 - zlo


def put_edges(which, rows, outer, inner):
    core, parity = place()[0], parity_of(which)
    for edge, last in ((outer, parity), (inner, 1 - parity)):
        start = pl.multiple_of((last ^ core) * BLK + last * (BLK - HALO), HALO)
        for kv in range(2):
            edge[kv] = rows(kv, pl.ds(start, HALO))


def rows_kernel(ci, x, out, low, high):
    low[...] = x[: BLK // 2, :]
    high[...] = x[BLK // 2 :, :]
    core, zlo = place()[:2]
    row = lax.broadcasted_iota(jnp.int32, (8, BLK), 0)
    col = lax.broadcasted_iota(jnp.int32, (8, BLK), 1)
    at = jnp.full((8, BLK), -1, jnp.int32)
    for r in range(4):
        at = jnp.where(row == r, ci[zlo, 4 * core + r] - core * BLK, at)
    hot = jnp.where(col == at, 1.0, 0.0).astype(BF16)
    got = jnp.dot(hot, x[...], preferred_element_type=F32)
    out[...] = got[:4].astype(BF16)


def context_rows(ci, x):
    return pl.pallas_call(
        rows_kernel,
        out_shape=(shape(4, D), shape(BLK // 2, D), shape(BLK // 2, D)),
        in_specs=[SM, VM],
        out_specs=(VM, VM, VM),
        compiler_params=params(4),
        name="context_rows",
    )(ci, x)


def context_kernel(c0, c1, c2, c3, gain, w, qkg, out, xs, normed):
    for j, c in enumerate((c0, c1, c2, c3)):
        xs[4 * j : 4 * j + 4, :] = c[...].astype(F32)
    v = xs[...]
    v = v * lax.rsqrt(jnp.mean(v * v, axis=-1, keepdims=True) + EPS)
    xs[...] = v

    def step(l, carry):
        normed[...] = (xs[...] * gain[pl.ds(l, 1), :]).astype(BF16)
        p = jnp.dot(normed[...], w[l, :, INNER:], preferred_element_type=F32)
        out[0, l, 0] = head_norm(p[:, :INNER], qkg[l, 1:2, :]).astype(BF16)
        out[0, l, 1] = p[:, INNER:].astype(BF16)
        return carry

    lax.fori_loop(0, 2, step, 0)


def context_kv(c, gain, w, qkg):
    return pl.pallas_call(
        context_kernel,
        out_shape=shape(1, 2, 2, 2 * CTX, INNER),
        in_specs=[VM] * 7,
        out_specs=VM,
        scratch_shapes=[
            pltpu.VMEM((2 * CTX, D), F32),
            pltpu.VMEM((2 * CTX, D), BF16),
        ],
        compiler_params=params(4),
        cost_estimate=pl.CostEstimate(
            flops=2 * 256 * D * 4 * INNER, transcendentals=0, bytes_accessed=8 * D * INNER
        ),
        name="context_kv",
    )(*c, gain, w, qkg)


def qkv_kernel(l, which, *refs):
    pieces, (gain, w, qkg, out, outer, inner, normed) = refs[:-7], refs[-7:]
    half = BLK // 2
    views = [p.at[pl.ds(r, half)] for p in pieces for r in range(0, p.shape[0], half)]
    norm_rows(views, gain.at[l : l + 1], normed)

    def put(m, c, p):
        out[c] = p

    project(normed, w, l, qkg, put, CLIP_TOK)
    put_edges(which, lambda kv, at: out[1 + kv, at, :], outer, inner)


def qkv(l, which, pieces, gain, w, qkg):
    return pl.pallas_call(
        functools.partial(qkv_kernel, l, which),
        out_shape=(
            shape(3, CLIP_TOK, INNER),
            shape(2, HALO, INNER),
            shape(2, HALO, INNER),
        ),
        in_specs=[VM] * (len(pieces) + 3),
        out_specs=(VM, VM, VM),
        scratch_shapes=[pltpu.VMEM((CLIP_TOK, D), BF16)],
        compiler_params=params(7),
        cost_estimate=pl.CostEstimate(
            flops=2 * CLIP_TOK * D * 3 * INNER,
            transcendentals=0,
            bytes_accessed=2 * (3 * D * INNER + CLIP_TOK * D),
        ),
        name="qkv",
    )(*pieces, gain, w, qkg)


def halo_mask(halo, which):
    parity = parity_of(which)
    seen = halo[parity]
    end = jnp.where(parity == 0, 0, lax.axis_size("clip") - 1)
    exists = jnp.where(lax.axis_index("clip") == end, 0, 1)
    lane = lax.broadcasted_iota(jnp.int32, (1, 2 * HALO), 1)
    mask = jnp.zeros((1, 2 * HALO), F32)
    for side, count in enumerate((seen, seen * exists)):
        prev = parity if side == 0 else 1 - parity
        low = side * HALO + prev * (HALO - 16 * count)
        mask = jnp.where(lane >= low, jnp.where(lane < low + 16 * count, 1.0, mask), mask)
    return mask


def attend_clip(cl, mask, mine, inner, outer, ctx, put, at=0):
    factor = math.log2(math.e) / math.sqrt(HD)
    tn = (((1,), (1,)), ((), ()))

    def step(h, carry):
        cols = pl.ds(pl.multiple_of(h * HD, HD), HD)
        q = mine[0, :, cols]
        rows = []
        for kv in range(2):
            parts = [mine[1 + kv, :, cols]]
            for ref in ctx:
                parts.append(ref[:, cl, kv, :, cols].reshape(-1, HD))
            rows.append(jnp.concatenate(parts, axis=0))
        k, v = rows
        kh = jnp.concatenate([inner[0, :, cols], outer[at, :, cols]], axis=0)
        vh = jnp.concatenate([inner[1, :, cols], outer[at + 1, :, cols]], axis=0)
        v = jnp.concatenate([v, jnp.ones_like(v)], axis=1)
        vh = jnp.concatenate([vh, jnp.ones_like(vh)], axis=1)
        s = lax.dot_general(q, k, tn, preferred_element_type=F32)
        sh = lax.dot_general(q, kh, tn, preferred_element_type=F32)
        p = jnp.exp2(s * factor).astype(BF16)
        ph = (jnp.exp2(sh * factor) * mask).astype(BF16)
        r = jnp.dot(p, v, preferred_element_type=F32)
        r = r + jnp.dot(ph, vh, preferred_element_type=F32)
        put(cols, (r[:, :HD] / r[:, HD:]).astype(BF16))
        return carry

    lax.fori_loop(0, HL, step, 0)


def attend_cost(clips, ctx):
    keys = CLIP_TOK + 2 * HALO + sum(c.shape[0] * c.shape[3] for c in ctx)
    return pl.CostEstimate(
        flops=clips * 6 * CLIP_TOK * keys * INNER,
        transcendentals=clips * HL * CLIP_TOK * keys,
        bytes_accessed=4 * keys * INNER + clips * 4 * CLIP_TOK * INNER,
    )


def attend_kernel(cl, which, halo, mine, inner, outer, c0, c1, c2, c3, out):
    def put(cols, a):
        out[0, :, cols] = a[:BLK]
        out[1, :, cols] = a[BLK:]

    ctx = (c0, c1, c2, c3)
    attend_clip(cl, halo_mask(halo, which), mine, inner, outer, ctx, put)


def attend(cl, which, halo, mine, inner, outer, ctx):
    return pl.pallas_call(
        functools.partial(attend_kernel, cl, which),
        out_shape=shape(2, BLK, INNER),
        in_specs=[SM] + [VM] * 7,
        out_specs=VM,
        compiler_params=params(7),
        cost_estimate=attend_cost(1, ctx),
        name="attend",
    )(halo, mine, inner, outer, *ctx)


def attend_pair_kernel(cl, at, *refs):
    (halo, qo, io, eo, qp, ip, ep) = refs[:7]
    ctx, (o0, o1, p0, p1) = refs[7:11], refs[11:]
    for which, args, (low, high) in (
        (0, (qo, ip, eo), (o0, o1)),
        (1, (qp, io, ep), (p0, p1)),
    ):

        def put(cols, a, low=low, high=high):
            low[:, cols] = a[:BLK]
            high[:, cols] = a[BLK:]

        attend_clip(cl, halo_mask(halo, which), *args, ctx, put, at)


def attend_pair(cl, at, halo, own, par, outer_own, outer_par, ctx):
    return pl.pallas_call(
        functools.partial(attend_pair_kernel, cl, at),
        out_shape=(shape(BLK, INNER),) * 4,
        in_specs=[SM] + [VM] * 10,
        out_specs=(VM,) * 4,
        compiler_params=params(7),
        cost_estimate=attend_cost(2, ctx),
        name="attend_pair",
    )(halo, own[0], own[2], outer_own, par[0], par[2], outer_par, *ctx)


def first_kernel(*refs):
    (o0, p0, o1, p1, o2, p2, o3, p3) = refs[:8]
    xs, refs = refs[8:-16], refs[-16:]
    (wslot, gain, w, qkg, ci) = refs[:5]
    (first, qo, eo, io, qp, ep, ip, ctx) = refs[5:13]
    (acat, xbuf, normed) = refs[13:]
    for j, (ao, ap) in enumerate(((o0, p0), (o1, p1), (p2, o2), (p3, o3))):
        for clip, piece in enumerate((ao, ap)):
            for b in range(2):
                row = (2 * clip + b) * BLK
                acat[row : row + BLK, j * INNER : (j + 1) * INNER] = piece[b ^ (j & 1)]
    rows = 2 * CLIP_TOK

    def block(k, carry):
        cols = pl.ds(quarter(place()[3], k), QUART)
        row = 0
        for x in xs:
            if row % CLIP_TOK == 0:
                left = acat[row : row + CLIP_TOK, :]
                t = jnp.dot(left, wslot[k], preferred_element_type=F32)
            end = row + x.shape[0]
            base = row - row % CLIP_TOK
            v = x[:, cols].astype(F32) + t[row - base : end - base]
            xbuf[row:end, cols] = v.astype(BF16)
            row = end
        return carry

    lax.fori_loop(0, 4, block, 0)
    first[...] = xbuf[:BLK, :]
    norm_rows([xbuf], gain.at[1:2], normed, 2)

    def put(m, c, p):
        @pl.when(m == 0)
        def _():
            qo[c] = p

        @pl.when(m == 1)
        def _():
            qp[c] = p

    project(normed, w, 1, qkg, put, rows)
    col = lax.broadcasted_iota(jnp.int32, (CLIP_TOK, CTX), 0)
    found = []
    for which, (q, e, i) in enumerate(((qo, eo, io), (qp, ep, ip))):
        put_edges(which, lambda kv, at, q=q: q[1 + kv, at, :], e, i)
        idx = jnp.where(parity_of(which) == 0, ci[0:1, :], ci[1:2, :])
        rel = ((idx // BLK) ^ place()[0]) * BLK + idx % BLK
        hot = jnp.where(col == rel, 1.0, 0.0).astype(BF16)
        tt = (((0,), (0,)), ((), ()))
        found.append(
            [
                lax.dot_general(hot, q[1 + kv], tt, preferred_element_type=F32)
                for kv in range(2)
            ]
        )
    for kv in range(2):
        both = jnp.concatenate([found[0][kv], found[1][kv]], axis=0)
        ctx[0, 0, kv] = both.astype(BF16)


def first_qkv(atts, xs, wslot, gain, w, qkg, ci):
    one = (
        shape(3, CLIP_TOK, INNER),
        shape(2, HALO, INNER),
        shape(2, HALO, INNER),
    )
    rows = 2 * CLIP_TOK
    res = pl.pallas_call(
        first_kernel,
        out_shape=(shape(BLK, D),) + one + one + (shape(1, 1, 2, 2 * CTX, INNER),),
        in_specs=[VM] * (13 + len(xs)),
        out_specs=(VM,) * 8,
        scratch_shapes=[
            pltpu.VMEM((rows, 4 * INNER), BF16),
            pltpu.VMEM((rows, D), BF16),
            pltpu.VMEM((rows, D), BF16),
        ],
        compiler_params=params(14),
        cost_estimate=pl.CostEstimate(
            flops=2 * rows * D * 7 * INNER,
            transcendentals=0,
            bytes_accessed=2 * (7 * D * INNER + 2 * rows * D),
        ),
        name="first_qkv",
    )(*atts, *xs, wslot, gain, w, qkg, ci)
    return res[0], res[1:4], res[4:7], res[7]


def final_kernel(*refs):
    skip, atts, others = refs[0], refs[1:5], refs[5:9]
    (xa, xb, first, wslot, out, acat) = refs[9:]
    for j in range(4):
        for b, piece in enumerate((atts[j], others[j])):
            acat[b * BLK : (b + 1) * BLK, j * INNER : (j + 1) * INNER] = piece[...]
    skip_first = skip[place()[1]] == 0

    def block(k, carry):
        cols = pl.ds(quarter(place()[2], k), QUART)
        t = jnp.dot(acat[...], wslot[k], preferred_element_type=F32)
        f = first[:, cols].astype(F32)
        strong = (f + t[:BLK]).astype(BF16).astype(F32)
        video = jnp.concatenate([xa[:, cols], xb[:, cols]], axis=0).astype(F32)
        other = (video + t[BLK:]).astype(BF16).astype(F32)
        weak = jnp.where(skip_first, other, f)
        out[:, cols] = (strong + GUIDE * (strong - weak)).astype(BF16)
        return carry

    lax.fori_loop(0, 4, block, 0)


def final(skip, atts, others, xa, xb, first, wslot):
    return pl.pallas_call(
        final_kernel,
        out_shape=shape(BLK, D),
        in_specs=[SM] + [VM] * 12,
        out_specs=VM,
        scratch_shapes=[pltpu.VMEM((2 * BLK, 4 * INNER), BF16)],
        compiler_params=params(7),
        cost_estimate=pl.CostEstimate(
            flops=4 * BLK * D * 4 * INNER,
            transcendentals=0,
            bytes_accessed=2 * (4 * D * INNER + 3 * BLK * D),
        ),
        name="final",
    )(skip, *atts, *others, xa, xb, first, wslot)


def after(value, *done):
    return lax.optimization_barrier((value,) + done)[0]


def columns_kernel(wo, *refs):
    outs, sems = refs[:2], refs[2]
    copies = []
    for l in range(2):
        cols = pl.ds(pl.multiple_of(place()[3 - l] * QUART, QUART), QUART)
        copies.append(
            pltpu.make_async_copy(wo.at[l, :, cols], outs[l], sems.at[l])
        )
    for copy in copies:
        copy.start()
    for copy in copies:
        copy.wait()


def columns(weight):
    return pl.pallas_call(
        columns_kernel,
        out_shape=(shape(INNER, QUART),) * 2,
        in_specs=[pl.BlockSpec(memory_space=pltpu.HBM)],
        out_specs=(VM, VM),
        scratch_shapes=[pltpu.SemaphoreType.DMA((2,))],
        compiler_params=params(3),
        name="columns",
    )(weight)


def edges(own, par):
    return send(par[1], edge_par), send(own[1], edge_own)


def body(video, norm_gain, w_qkv, qk_gain, w_out, skip_layer, halo_frames, context_index):
    x0 = video
    piece0, piece1 = columns(pltpu.with_memory_space_constraint(w_out, pltpu.HBM))
    here0 = send(piece0, to_far_z)
    c0, xa, xb = context_rows(context_index, after(x0, piece0))
    c = [c0, send(c0, to_sib), send(c0, to_z), send(c0, to_diag)]
    x2a = send(xa, to_z)
    x1 = send(after(x0, c0), to_sib)
    w = stage(pltpu.with_memory_space_constraint(jnp.transpose(w_qkv, (0, 2, 1, 3)), pltpu.HBM))
    kv = context_kv(c, norm_gain, w, qk_gain)
    kz = send(kv, to_far)
    x2b = send(after(xb, kv), to_z)
    wz0 = [here0] + [send(after(here0, kv), to_y(d)) for d in (1, 3)]
    own0 = qkv(0, 0, (after(xa, kv), xb, x1), norm_gain, w, qk_gain)
    kx = pack(kv, after(kz, own0[0]))
    kxs = [send(kx, to_x(d)) for d in (1, 3, 2)]
    x3a = send(after(x2a, kx), to_sib)
    own1 = qkv(1, 0, (after(xa, kx), xb, x1), norm_gain, w, qk_gain)
    ky = pack(kx, *[after(k, own1[0]) for k in kxs])
    kys = [send(ky, to_y(d)) for d in (1, 3, 2)]
    here1 = send(after(piece1, ky), to_far_z)
    x3b = send(after(x2b, own1[0]), to_sib)
    halves = (after(x2a, ky), x2b, x3a, x3b)
    par0 = qkv(0, 1, halves, norm_gain, w, qk_gain)
    eo, ep = edges((None, after(own0[1], par0[0])), par0)
    wsib = send(after(w_out, par0[0]), to_sib)
    ctx = [ky] + kys
    ao = attend(0, 0, halo_frames, own0[0], par0[2], eo, ctx)
    wz0.append(send(after(here0, ao), to_y(2)))
    oz = send(ao, to_z)
    os = send(ao, to_sib)
    ap = attend(0, 1, halo_frames, after(par0[0], ao), own0[2], ep, ctx)
    pz = send(ap, to_z)
    ps = send(ap, to_sib)
    halves = (after(x2a, ap), x2b, x3a, x3b)
    par1 = qkv(1, 1, halves, norm_gain, w, qk_gain)
    wzs0 = [send(after(p, ap), to_sib) for p in wz0[:3]]
    wz1 = [here1] + [send(after(here1, par1[0]), to_x(d)) for d in (1, 3, 2)]
    wzs0.append(send(after(wz0[3], par1[0]), to_sib))
    ozs = send(after(oz, par1[0]), to_sib)
    wslot0 = assemble(0, after(w_out, par1[0]), wsib, wz0, wzs0)
    pzs = send(pz, to_sib)

    first, fo, fp, fkv = first_qkv(
        (ao, ap, os, ps, oz, pz, ozs, pzs),
        (xa, xb, x1, x2a, x2b, x3a, x3b),
        wslot0,
        norm_gain,
        w,
        qk_gain,
        context_index,
    )
    fz = send(fkv, to_far)
    both_own = pack(own1[1], fo[1])
    both_par = pack(par1[1], fp[1])
    fx = pack(fkv, fz)
    fxs = [send(fx, to_x(d)) for d in (1, 3, 2)]
    sp = send(both_own, edge_own)
    so = send(after(both_par, fx), edge_par)
    fy = pack(fx, *fxs)
    fys = [send(fy, to_y(d)) for d in (1, 3, 2)]
    mine = (after(own1[0], fy),) + own1[1:]
    b = attend_pair(1, 0, halo_frames, mine, par1, so, sp, ctx)
    others = [b[0], send(b[1], to_sib), send(b[2], to_z), send(b[3], to_diag)]
    mine = (after(fo[0], b[0]),) + fo[1:]
    g = attend_pair(0, 2, halo_frames, mine, fp, so, sp, [fy] + fys)
    atts = [g[0], send(g[1], to_sib), send(g[2], to_z), send(g[3], to_diag)]
    wzs1 = [send(after(p, b[0]), to_sib) for p in wz1]
    wslot1 = assemble(1, after(w_out, g[0]), wsib, wz1, wzs1)
    return final(skip_layer, atts, others, xa, xb, first, wslot1)


def solution(mesh):
    in_specs = (
        P(("clip", "head"), None),
        P(),
        P(None, None, None, "head"),
        P(),
        P(None, "head", None),
        P("clip"),
        P("clip"),
        P("clip", None),
    )
    out_specs = P(("clip", "head"), None)

    return jax.shard_map(
        body, mesh=mesh, in_specs=in_specs, out_specs=out_specs, check_vma=False
    )
```
